32 devices in a mesh: seq: 2 (over y), fsdp: 16 (over z, x, core).
Axes of the slice: x: 2, y: 2, z: 4, core: 2. Of those that a mesh axis runs over, the one named last changes fastest.
Arguments:
- tokens: bfloat16 [16, 1024, 1024], P('fsdp', 'seq'), may hold values from -6 to 6
- blocks: int32 [16, 1024], P('fsdp'), may hold values from 0 to 7, never falling along the last dimension, each value on 1 to 256 neighbouring positions
- first_gain: bfloat16 [1024], P('fsdp'), may hold values from 0.5 to 1.5
- first_shift: bfloat16 [1024], P('fsdp'), may hold values from -1.5 to 1.5
- joint_weight: bfloat16 [1024, 3072], P('fsdp'), may hold values from -0.1875 to 0.1875
- joint_bias: bfloat16 [2, 1024], P(None, 'fsdp'), may hold values from -1.5 to 1.5
- output_weight: bfloat16 [1024, 1024], P('fsdp'), may hold values from -0.75 to 0.75
- output_bias: bfloat16 [1024], P('fsdp'), may hold values from -1.5 to 1.5
- second_gain: bfloat16 [1024], P('fsdp'), may hold values from 0.5 to 1.5
- second_shift: bfloat16 [1024], P('fsdp'), may hold values from -1.5 to 1.5
- upward_weight: bfloat16 [1024, 4096], P('fsdp'), may hold values from -0.1875 to 0.1875
- upward_bias: bfloat16 [4096], P('fsdp'), may hold values from -1.5 to 1.5
- downward_weight: bfloat16 [4096, 1024], P('fsdp'), may hold values from -0.125 to 0.125
- downward_bias: bfloat16 [1024], P('fsdp'), may hold values from -1.5 to 1.5
- cotangent: bfloat16 [16, 1024, 1024], P('fsdp', 'seq'), may hold values from -6 to 6
Outputs:
- result: bfloat16 [16, 1024, 1024], P('fsdp', 'seq')
- grad_tokens: float32 [16, 1024, 1024], P('fsdp', 'seq')
- grad_first_gain: float32 [1024], P('fsdp')
- grad_first_shift: float32 [1024], P('fsdp')
- grad_joint_weight: float32 [1024, 3072], P('fsdp')
- grad_joint_bias: float32 [2, 1024], P(None, 'fsdp')
- grad_output_weight: float32 [1024, 1024], P('fsdp')
- grad_output_bias: float32 [1024], P('fsdp')
- grad_second_gain: float32 [1024], P('fsdp')
- grad_second_shift: float32 [1024], P('fsdp')
- grad_upward_weight: float32 [1024, 4096], P('fsdp')
- grad_upward_bias: float32 [4096], P('fsdp')
- grad_downward_weight: float32 [4096, 1024], P('fsdp')
- grad_downward_bias: float32 [1024], P('fsdp')
The draws below stay inside these ranges and needn't reach their ends.
Inputs may be any that keep to these rules, and one draw needn't show every extreme that they name: `blocks`: along each sequence the block number never falls; every block has 1 to 256 tokens, and one has exactly 256.
All inputs are finite; a program needn't handle non-finite values.
Results may differ from the reference program's by a relative error of at most 0.014.
Values may be sent and summed in bfloat16 or wider, within the bound.
No kernel may reach another device: no remote copies, remote signals or barrier semaphores. Data moves between devices by JAX's collectives and lax.ppermute only.
A program may use at most 192 MiB of HBM per device.

```python
import math
import jax
import jax.numpy as jnp
import numpy as np
from jax import lax

D = 1024
HEADS = 16
HEAD_DIM = 64
FF = 4096
BLOCK = 256
LEN = 1024
SEQS = 16


def levels(stream_key, shape, split, low, high):
    level, own = 1.0, jax.random.fold_in(stream_key, 6)
    for dim, parts in split:
        steps = jnp.exp(jax.random.uniform(jax.random.fold_in(own, dim), (parts,), jnp.float32, low / len(split), high / len(split)))
        level = level * jnp.repeat(steps, shape[dim] // parts).reshape([-1 if axis == dim else 1 for axis in range(len(shape))])
    return level


def length_profile(number_of, total, limit, skew):
    weights = [(1 << 20) // math.isqrt(rank ** skew) + 1 for rank in range(2, number_of + 1)]
    rest, given = total - limit - (number_of - 1), [1] * (number_of - 1)
    while rest > 0:
        free = [i for i in range(number_of - 1) if given[i] < limit]
        pool, remaining = sum([weights[i] for i in free]), rest
        for i in free:
            addition = min(limit - given[i], max(1, remaining * weights[i] // pool), rest)
            given[i] = given[i] + addition
            rest = rest - addition
    return np.array([limit] + given)


def uneven_parts(rng, count, total, bound, slope):
    if count == 2:
        one = jax.random.randint(rng, (), max(1, total - bound), min(bound, total - 1) + 1)
        return jnp.stack([one, total - one])
    lengths = jnp.asarray(length_profile(count, total, bound, slope), jnp.int32)
    pairs = (count - 1) // 2
    donor, sink = lengths[1:1 + 2 * pairs:2], lengths[2:2 + 2 * pairs:2]
    margin = jnp.minimum(donor - 1, bound - sink)
    shifted = jax.random.randint(jax.random.fold_in(rng, 1), (pairs,), 0, 1 << 20) % (margin + 1)
    lengths = lengths.at[1:1 + 2 * pairs:2].set(donor - shifted).at[2:2 + 2 * pairs:2].set(sink + shifted)
    return lengths[jax.random.permutation(jax.random.fold_in(rng, 2), count)]


def scatter_about(stream_key, dims, scale, reach, split=(), held_as=jnp.bfloat16):
    result = scale * jax.random.normal(stream_key, dims, jnp.float32)
    if split:
        result = result * levels(stream_key, dims, split, -0.22, 0.18)
    return jnp.clip(result, -reach, reach).astype(held_as)


def setup_inputs(seed: int = 0) -> dict:
    key_of = jax.random.split(jax.random.key(seed), 16)
    tokens = scatter_about(key_of[0], (SEQS, LEN, D), 1.0, 6.0, ((0, 16), (1, 2)))
    blocks = jax.vmap(lambda own: jnp.searchsorted(jnp.cumsum(uneven_parts(own, 2 * LEN // BLOCK, LEN, BLOCK, 1)), jnp.arange(LEN), side="right"))(jax.random.split(key_of[1], SEQS)).reshape((SEQS, LEN)).astype(jnp.int32)
    first_gain = jnp.clip(1.0 + 0.1 * jax.random.normal(key_of[2], (D,), jnp.float32), 0.5, 1.5).astype(jnp.bfloat16)
    first_shift = scatter_about(key_of[3], (D,), 0.3, 1.5, ((0, 16),))
    joint_weight = scatter_about(key_of[4], (D, 3 * D), D ** -0.5, 0.1875, ((0, 16),))
    joint_bias = scatter_about(key_of[5], (2, D), 0.3, 1.5, ((1, 16),))
    output_weight = scatter_about(key_of[6], (D, D), (D // 16) ** -0.5, 0.75, ((0, 16),))
    output_bias = scatter_about(key_of[7], (D,), 0.3, 1.5, ((0, 16),))
    second_gain = jnp.clip(1.0 + 0.1 * jax.random.normal(key_of[8], (D,), jnp.float32), 0.5, 1.5).astype(jnp.bfloat16)
    second_shift = scatter_about(key_of[9], (D,), 0.3, 1.5, ((0, 16),))
    upward_weight = scatter_about(key_of[10], (D, FF), D ** -0.5, 0.1875, ((0, 16),))
    upward_bias = scatter_about(key_of[11], (FF,), 0.3, 1.5, ((0, 16),))
    downward_weight = scatter_about(key_of[12], (FF, D), (FF // 2) ** -0.5, 0.125, ((0, 16),))
    downward_bias = scatter_about(key_of[13], (D,), 0.3, 1.5, ((0, 16),))
    cotangent = scatter_about(key_of[14], (SEQS, LEN, D), 1.0, 6.0, ((0, 16), (1, 2)))
    return dict(tokens=tokens, blocks=blocks, first_gain=first_gain, first_shift=first_shift, joint_weight=joint_weight, joint_bias=joint_bias, output_weight=output_weight, output_bias=output_bias, second_gain=second_gain, second_shift=second_shift, upward_weight=upward_weight, upward_bias=upward_bias, downward_weight=downward_weight, downward_bias=downward_bias, cotangent=cotangent)


@jax.custom_vjp
def low(v):
    return lax.optimization_barrier(v.astype(jnp.bfloat16)).astype(jnp.float32)

@jax.custom_vjp
def low_back(v):
    return v

def low_keep(v):
    return (low(v), None)

def low_pass(kept, grad):
    return (grad,)

def back_keep(v):
    return (v, None)

def back_low(kept, grad):
    return (low(grad),)
low.defvjp(low_keep, low_pass)
low_back.defvjp(back_keep, back_low)
EPSILON = 1e-05
HIGHEST = lax.Precision.HIGHEST

def layer_norm(values, gain, shift):
    center = values - lax.optimization_barrier(jnp.mean(values, axis=-1, keepdims=True))
    spread = lax.optimization_barrier(jnp.mean(center * center, axis=-1, keepdims=True))
    return center * lax.rsqrt(spread + EPSILON) * gain + shift

def attend(packed):
    joint_row, block_row = packed
    heads = joint_row.reshape(LEN, 3, HEADS, HEAD_DIM)
    positions = jnp.arange(LEN)
    distance = jnp.abs(positions[:, None] - positions[None, :]).astype(jnp.float32)
    allowed = block_row[None, :] <= block_row[:, None]
    slopes = jnp.exp2(-8.0 * (jnp.arange(HEADS).astype(jnp.float32) + 1.0) / HEADS)
    scores = jnp.einsum('qhd,khd->hqk', heads[:, 0], heads[:, 1], precision=HIGHEST) * HEAD_DIM ** (-0.5)
    scores = scores - slopes[:, None, None] * distance
    scores = low_back(scores)
    scores = jnp.where(allowed, scores, -1e+30)
    probs = low(jax.nn.softmax(scores, axis=-1))
    mixed = jnp.einsum('hqk,khd->qhd', probs, heads[:, 2], precision=HIGHEST)
    return mixed.reshape(LEN, D)

def forward(blocks, tokens, first_gain, first_shift, joint_weight, joint_bias, output_weight, output_bias, second_gain, second_shift, upward_weight, upward_bias, downward_weight, downward_bias):
    inputs = tokens.reshape(-1, D)
    normed_one = low(layer_norm(inputs, first_gain, first_shift))
    bias_full = jnp.concatenate([joint_bias[0], jnp.zeros((D,), jnp.float32), joint_bias[1]])
    joint = jnp.dot(normed_one, joint_weight, precision=HIGHEST) + bias_full
    joint = low_back(low(joint))
    mixed = lax.map(jax.checkpoint(attend), (joint.reshape(SEQS, LEN, 3 * D), blocks))
    mixed = low_back(low(mixed.reshape(-1, D)))
    branch = low_back(jnp.dot(mixed, output_weight, precision=HIGHEST) + output_bias)
    hidden = inputs + branch
    normed_two = low(layer_norm(hidden, second_gain, second_shift))
    upward = low_back(jnp.dot(normed_two, upward_weight, precision=HIGHEST) + upward_bias)
    activated = low(jax.nn.gelu(upward, approximate=True))
    branch_two = low_back(jnp.dot(activated, downward_weight, precision=HIGHEST) + downward_bias)
    return (hidden + branch_two).reshape(SEQS, LEN, D)

def reference(tokens, blocks, first_gain, first_shift, joint_weight, joint_bias, output_weight, output_bias, second_gain, second_shift, upward_weight, upward_bias, downward_weight, downward_bias, cotangent):
    floats = [value.astype(jnp.float32) for value in (tokens, first_gain, first_shift, joint_weight, joint_bias, output_weight, output_bias, second_gain, second_shift, upward_weight, upward_bias, downward_weight, downward_bias)]

    def runner(*values):
        return forward(blocks, *values)
    output, puller = jax.vjp(runner, *floats)
    grads = puller(cotangent.astype(jnp.float32))
    return (output.astype(jnp.bfloat16), grads[0], grads[1], grads[2], grads[3], grads[4], grads[5], grads[6], grads[7], grads[8], grads[9], grads[10], grads[11], grads[12])
```

```python
import jax
import jax.numpy as jnp
from jax import lax
from jax.experimental import pallas as pl
from jax.experimental.pallas import tpu as pltpu
from jax.sharding import PartitionSpec as P

HEADS = 16
HEAD_DIM = 64
TILE = 256
EPSILON = 1e-05
FAR = 1e30


def gelu_tanh(values):
    return jax.nn.gelu(values, approximate=True)


def matmul(left, right):
    return jnp.dot(left, right, preferred_element_type=jnp.float32)


def left_contract(left, right):
    return lax.dot_general(
        left, right, (((0,), (0,)), ((), ())), preferred_element_type=jnp.float32
    )


def right_contract(left, right):
    return lax.dot_general(
        left, right, (((1,), (1,)), ((), ())), preferred_element_type=jnp.float32
    )


def standardize(values):
    center = values - jnp.mean(values, axis=-1, keepdims=True)
    spread = jnp.mean(center * center, axis=-1, keepdims=True)
    rate = lax.rsqrt(spread + EPSILON)
    return center * rate, rate


def norm_back(grad, gain, xhat, rate):
    e = grad * gain
    mean_e = jnp.mean(e, axis=-1, keepdims=True)
    mean_ex = jnp.mean(e * xhat, axis=-1, keepdims=True)
    return (e - mean_e - xhat * mean_ex) * rate


def half_starts(side, half):
    first = pl.multiple_of(side * half, half)
    second = pl.multiple_of(half - side * half, half)
    return first, second


def in_order(ref, first, second, half):
    return jnp.concatenate([ref[pl.ds(first, half), :], ref[pl.ds(second, half), :]], axis=0)


def tile_start(g, first, second, half):
    per_half = half // TILE
    base = first if g < per_half else second
    return pl.multiple_of(base + (g % per_half) * TILE, TILE)


def pad_head(x, a):
    zeros = jnp.zeros((HEAD_DIM, x.shape[1]), x.dtype)
    mine = x[a * HEAD_DIM : (a + 1) * HEAD_DIM]
    return jnp.concatenate([mine, zeros] if a == 0 else [zeros, mine], axis=0)


def attend_kernel(side_ref, slope_ref, q_ref, k_ref, v_ref, far_ref, out_ref, log_ref):
    length = q_ref.shape[0]
    half = length // 2
    pair = pl.program_id(0)
    first, second = half_starts(side_ref[0], half)
    keys = in_order(k_ref, first, second, half)
    values_t = in_order(v_ref, first, second, half).T
    for g in range(length // TILE):
        reach = min((g + 2) * TILE, length)
        start = tile_start(g, first, second, half)
        queries_t = (q_ref[pl.ds(start, TILE), :] * jnp.bfloat16(HEAD_DIM ** (-0.5))).T
        pieces = []
        for a in range(2):
            slope = slope_ref[2 * pair + a]
            scores = matmul(keys[:reach], pad_head(queries_t, a))
            scores = scores - slope * far_ref[:reach, g * TILE : (g + 1) * TILE]
            top = jnp.max(scores, axis=0, keepdims=True)
            weights = jnp.exp(scores - top)
            total = jnp.sum(weights, axis=0, keepdims=True)
            mixed_t = matmul(
                values_t[a * HEAD_DIM : (a + 1) * HEAD_DIM, :reach], weights.astype(jnp.bfloat16)
            )
            pieces.append(mixed_t / total)
            log_ref[0, a : a + 1, g * TILE : (g + 1) * TILE] = top + jnp.log(total)
        out_ref[pl.ds(start, TILE), :] = jnp.concatenate(pieces, axis=0).T.astype(jnp.bfloat16)


def attend_heads(joint, side, slopes, far):
    length, width = joint.shape
    pairs = width // 3 // 128
    whole = lambda offset: pl.BlockSpec((length, 128), lambda p, s: (0, p + offset))
    return pl.pallas_call(
        attend_kernel,
        grid_spec=pltpu.PrefetchScalarGridSpec(
            num_scalar_prefetch=1,
            grid=(pairs,),
            in_specs=[
                pl.BlockSpec(memory_space=pltpu.SMEM),
                whole(0),
                whole(pairs),
                whole(2 * pairs),
                pl.BlockSpec((length, length), lambda p, s: (0, 0)),
            ],
            out_specs=[
                pl.BlockSpec((length, 128), lambda p, s: (0, p)),
                pl.BlockSpec((1, 2, length), lambda p, s: (p, 0, 0)),
            ],
        ),
        out_shape=[
            jax.ShapeDtypeStruct((length, width // 3), jnp.bfloat16),
            jax.ShapeDtypeStruct((pairs, 2, length), jnp.float32),
        ],
        compiler_params=pltpu.CompilerParams(vmem_limit_bytes=48 << 20),
        name="attend",
    )(side, slopes, joint, joint, joint, far)


def back_kernel(
    side_ref,
    slope_ref,
    q_ref,
    k_ref,
    v_ref,
    far_ref,
    log_ref,
    mixed_ref,
    grad_ref,
    out_ref,
    dq_ref,
    dk_ref,
    dv_ref,
):
    length = q_ref.shape[0]
    half = length // 2
    pair = pl.program_id(0)
    part = pl.program_id(1)
    first, second = half_starts(side_ref[0], half)
    factor = HEAD_DIM ** (-0.5)

    @pl.when(part == 0)
    def _():
        keys = in_order(k_ref, first, second, half)
        keys_t = keys.T
        values = in_order(v_ref, first, second, half)
        lane = lax.broadcasted_iota(jnp.int32, (TILE, 128), 1)
        dk_ref[...] = jnp.zeros_like(dk_ref)
        dv_ref[...] = jnp.zeros_like(dv_ref)
        for g in range(length // TILE):
            reach = min((g + 2) * TILE, length)
            start = tile_start(g, first, second, half)
            queries = q_ref[pl.ds(start, TILE), :] * jnp.bfloat16(factor)
            queries_t = queries.T
            grads = grad_ref[pl.ds(start, TILE), :]
            grads_t = grads.T
            product = grads.astype(jnp.float32) * mixed_ref[pl.ds(start, TILE), :].astype(
                jnp.float32
            )
            product_t = product.T
            pieces = []
            for a in range(2):
                rows = slice(a * HEAD_DIM, (a + 1) * HEAD_DIM)
                slope = slope_ref[2 * pair + a]
                own = (lane < HEAD_DIM) if a == 0 else (lane >= HEAD_DIM)
                scores = matmul(keys[:reach], pad_head(queries_t, a))
                scores = scores - slope * far_ref[:reach, g * TILE : (g + 1) * TILE]
                probs = jnp.exp(scores - log_ref[0, a : a + 1, g * TILE : (g + 1) * TILE])
                grad_probs = matmul(values[:reach], pad_head(grads_t, a))
                inner = jnp.sum(product_t[rows], axis=0, keepdims=True)
                grad_scores = (probs * (grad_probs - inner)).astype(jnp.bfloat16)
                zero = jnp.zeros((), jnp.bfloat16)
                dk_ref[:reach] += matmul(grad_scores, jnp.where(own, queries, zero))
                dv_ref[:reach] += matmul(probs.astype(jnp.bfloat16), jnp.where(own, grads, zero))
                pieces.append(matmul(keys_t[rows, :reach], grad_scores))
            both = jnp.concatenate(pieces, axis=0).T * factor
            dq_ref[pl.ds(start, TILE), :] = both.astype(jnp.bfloat16)
        out_ref[...] = dq_ref[...]

    @pl.when(part == 1)
    def _():
        out_ref[pl.ds(first, half), :] = dk_ref[:half].astype(jnp.bfloat16)
        out_ref[pl.ds(second, half), :] = dk_ref[half:].astype(jnp.bfloat16)

    @pl.when(part == 2)
    def _():
        out_ref[pl.ds(first, half), :] = dv_ref[:half].astype(jnp.bfloat16)
        out_ref[pl.ds(second, half), :] = dv_ref[half:].astype(jnp.bfloat16)


def attend_back(joint, side, slopes, far, logs, mixed, grads):
    length, width = joint.shape
    pairs = width // 3 // 128
    whole = lambda offset: pl.BlockSpec((length, 128), lambda p, t, s: (0, p + offset))
    return pl.pallas_call(
        back_kernel,
        grid_spec=pltpu.PrefetchScalarGridSpec(
            num_scalar_prefetch=1,
            grid=(pairs, 3),
            in_specs=[
                pl.BlockSpec(memory_space=pltpu.SMEM),
                whole(0),
                whole(pairs),
                whole(2 * pairs),
                pl.BlockSpec((length, length), lambda p, t, s: (0, 0)),
                pl.BlockSpec((1, 2, length), lambda p, t, s: (p, 0, 0)),
                whole(0),
                whole(0),
            ],
            out_specs=pl.BlockSpec((length, 128), lambda p, t, s: (0, t * pairs + p)),
            scratch_shapes=[
                pltpu.VMEM((length, 128), jnp.bfloat16),
                pltpu.VMEM((length, 128), jnp.float32),
                pltpu.VMEM((length, 128), jnp.float32),
            ],
        ),
        out_shape=jax.ShapeDtypeStruct((length, width), jnp.bfloat16),
        compiler_params=pltpu.CompilerParams(vmem_limit_bytes=48 << 20),
        name="attend_back",
    )(side, slopes, joint, joint, joint, far, logs, mixed, grads)


def per_device(
    tokens,
    blocks,
    first_gain,
    first_shift,
    joint_weight,
    joint_bias,
    output_weight,
    output_bias,
    second_gain,
    second_shift,
    upward_weight,
    upward_bias,
    downward_weight,
    downward_bias,
    cotangent,
):
    groups = lax.axis_size("seq")
    shards = lax.axis_size("fsdp")
    side = lax.axis_index("seq")
    half_tokens = tokens.shape[1]
    width = tokens.shape[2]
    rows = joint_weight.shape[0]
    length = half_tokens * groups
    local_heads = HEADS // groups
    part = width // groups
    hidden_rows = downward_weight.shape[0]
    unit = hidden_rows // groups
    wide = 3 * part
    f32 = jnp.float32
    bf16 = jnp.bfloat16

    def swap(x):
        return lax.ppermute(x, "seq", [(s, groups - 1 - s) for s in range(groups)])

    def pick(x, axis, which=side):
        return lax.dynamic_index_in_dim(x, which, axis, keepdims=False)

    def gather(x):
        return lax.all_gather(x, "fsdp", axis=0, tiled=True)

    def scatter(x):
        return lax.psum_scatter(x, "fsdp", scatter_dimension=0, tiled=True)

    def weave(own, other, axis):
        return jnp.where(
            side == 0, jnp.stack([own, other], axis), jnp.stack([other, own], axis)
        )

    token_own = tokens[0]
    grad_own = cotangent[0]
    token_other = swap(token_own)
    grad_other = swap(grad_own)

    vectors = jnp.concatenate(
        [
            first_gain,
            first_shift,
            joint_bias[0],
            joint_bias[1],
            output_bias,
            second_gain,
            second_shift,
            downward_bias,
            upward_bias,
        ]
    )
    vector_rows = 16
    vector_block = jnp.pad(
        vectors[None], ((0, vector_rows - 1), (0, wide - vectors.shape[0]))
    )
    joint_part = pick(joint_weight.reshape(rows, 3, groups, part), 2).reshape(rows, wide)
    packed = gather(jnp.concatenate([joint_part, vector_block], axis=0))
    packed = packed.reshape(shards, rows + vector_rows, wide)
    joint_full = packed[:, :rows].reshape(width, wide)
    vector_full = packed[:, rows].astype(f32)
    out_full = gather(output_weight)
    up_part = pick(upward_weight.reshape(rows, shards, groups, unit), 2)
    up_full = gather(up_part.reshape(rows, shards * unit))
    down_full = gather(pick(downward_weight.reshape(groups, unit, width), 0))

    def vector(index):
        return vector_full[:, index * rows : (index + 1) * rows].reshape(width)

    gain_one, shift_one, query_bias, value_bias = (vector(n) for n in range(4))
    out_bias, gain_two, shift_two, down_bias = (vector(n) for n in range(4, 8))
    up_bias = vector_full[:, 8 * rows : 8 * rows + hidden_rows].reshape(shards, groups, unit)
    up_bias = pick(up_bias, 1).reshape(shards * unit)
    joint_bias_part = jnp.concatenate(
        [
            pick(query_bias.reshape(groups, part), 0),
            jnp.zeros((part,), f32),
            pick(value_bias.reshape(groups, part), 0),
        ]
    )

    inputs = jnp.concatenate([token_own, token_other], axis=0).astype(f32)
    xhat_one, rate_one = standardize(inputs)
    normed_one = (xhat_one * gain_one + shift_one).astype(bf16)
    joint = (matmul(normed_one, joint_full) + joint_bias_part).astype(bf16)

    positions = jnp.arange(length)
    distance = jnp.abs(positions[:, None] - positions[None, :]).astype(f32)
    block_row = blocks[0]
    far = jnp.where(block_row[:, None] <= block_row[None, :], distance, FAR)
    head_index = side * local_heads + jnp.arange(local_heads)
    slopes = jnp.exp2(-8.0 * (head_index.astype(f32) + 1.0) / HEADS)
    side_array = side.astype(jnp.int32).reshape(1)
    mixed_own, logs = attend_heads(joint, side_array, slopes, far)

    mixed_other = swap(mixed_own)
    mixed_other = jnp.concatenate([mixed_other[half_tokens:], mixed_other[:half_tokens]], axis=0)
    mixed = jnp.concatenate([mixed_own, mixed_other], axis=1)
    out_parts = out_full.reshape(groups, part, width)
    out_turned = jnp.concatenate([pick(out_parts, 0), pick(out_parts, 0, groups - 1 - side)], axis=0)
    hidden = inputs + matmul(mixed, out_turned) + out_bias
    xhat_two, rate_two = standardize(hidden)
    normed_two = (xhat_two * gain_two + shift_two).astype(bf16)
    upward = matmul(normed_two, up_full) + up_bias
    activated = gelu_tanh(upward).astype(bf16)

    grad_low = jnp.concatenate([grad_own, grad_other], axis=0)
    grad_down = left_contract(activated, grad_low).astype(bf16)
    grad_down = scatter(grad_down)
    grad_act = right_contract(grad_low, down_full)
    grad_up = jax.vjp(gelu_tanh, upward)[1](grad_act)[0].astype(bf16)
    grad_up_weight = scatter(left_contract(normed_two, grad_up).astype(bf16))
    grad_two = right_contract(grad_up, up_full)
    grad_two_own = grad_two[:half_tokens] + swap(grad_two[half_tokens:].astype(bf16)).astype(f32)
    grad_hidden = grad_own.astype(f32) + norm_back(
        grad_two_own, gain_two, xhat_two[:half_tokens], rate_two[:half_tokens]
    )
    hidden_low = grad_hidden.astype(bf16)

    grad_mixed = right_contract(hidden_low, out_turned).astype(bf16)
    grad_heads = jnp.concatenate([grad_mixed[:, :part], swap(grad_mixed[:, part:])], axis=0)
    grad_joint = attend_back(joint, side_array, slopes, far, logs, mixed_own, grad_heads)

    low_parts = hidden_low.reshape(half_tokens, groups, part)
    low_columns = jnp.concatenate(
        [pick(low_parts, 1), swap(pick(low_parts, 1, groups - 1 - side))], axis=0
    )
    grad_out = left_contract(mixed, low_columns).astype(bf16)
    out_rows = grad_out.reshape(groups, part, part)
    grad_out = jnp.concatenate([pick(out_rows, 0), pick(out_rows, 0, groups - 1 - side)], axis=0)
    grad_out = scatter(grad_out)

    partial_out = matmul(activated, down_full)
    result_other = swap(partial_out[half_tokens:].astype(bf16)).astype(f32)
    result = hidden[:half_tokens] + partial_out[:half_tokens] + result_other + down_bias

    grad_joint_weight = left_contract(normed_one, grad_joint).astype(bf16)
    grad_one = right_contract(grad_joint, joint_full)

    def spread(x):
        empty = jnp.zeros_like(x)
        return weave(x, empty, 0).reshape(width)

    joint_sums = jnp.sum(grad_joint.astype(f32), axis=0)
    sums = [
        jnp.sum(grad_one * xhat_one, axis=0),
        jnp.sum(grad_one, axis=0),
        spread(joint_sums[:part]),
        spread(joint_sums[2 * part :]),
        jnp.sum(hidden_low.astype(f32), axis=0),
        jnp.sum(grad_two * xhat_two, axis=0),
        jnp.sum(grad_two, axis=0),
        jnp.sum(grad_own.astype(f32), axis=0),
    ]
    up_sums = jnp.sum(grad_up.astype(f32), axis=0).reshape(shards, unit)
    up_sums = weave(up_sums, jnp.zeros_like(up_sums), 1).reshape(shards, hidden_rows)
    sum_rows = jnp.concatenate([s.reshape(shards, rows) for s in sums] + [up_sums], axis=1)
    sum_rows = sum_rows.astype(bf16)
    sum_block = jnp.pad(
        sum_rows[:, None],
        ((0, 0), (0, vector_rows - 1), (0, wide - sum_rows.shape[1])),
    )
    last = jnp.concatenate([grad_joint_weight.reshape(shards, rows, wide), sum_block], axis=1)
    last = scatter(last.reshape(shards * (rows + vector_rows), wide))

    grad_one_own = grad_one[:half_tokens] + swap(grad_one[half_tokens:].astype(bf16)).astype(f32)
    grad_tokens = grad_hidden + norm_back(
        grad_one_own, gain_one, xhat_one[:half_tokens], rate_one[:half_tokens]
    )

    down_total = weave(grad_down, swap(grad_down), 0).reshape(hidden_rows, width)
    up_own = grad_up_weight.reshape(rows, shards, unit)
    up_other = swap(grad_up_weight).reshape(rows, shards, unit)
    up_total = weave(up_own, up_other, 2).reshape(rows, shards * hidden_rows)
    out_total = weave(grad_out, swap(grad_out), 1).reshape(rows, width)
    last_other = swap(last)
    joint_total = weave(
        last[:rows].reshape(rows, 3, part), last_other[:rows].reshape(rows, 3, part), 2
    ).reshape(rows, 3 * width)
    vector_total = last[rows].astype(f32) + last_other[rows].astype(f32)

    def total(index):
        return vector_total[index * rows : (index + 1) * rows]

    return (
        result.astype(bf16)[None],
        grad_tokens[None],
        total(0),
        total(1),
        joint_total.astype(f32),
        jnp.stack([total(2), total(3)]),
        out_total.astype(f32),
        total(4),
        total(5),
        total(6),
        up_total.astype(f32),
        vector_total[8 * rows : 8 * rows + hidden_rows],
        down_total.astype(f32),
        total(7),
    )


def solution(mesh):
    in_specs = (
        P("fsdp", "seq", None),
        P("fsdp", None),
        P("fsdp"),
        P("fsdp"),
        P("fsdp", None),
        P(None, "fsdp"),
        P("fsdp", None),
        P("fsdp"),
        P("fsdp"),
        P("fsdp"),
        P("fsdp", None),
        P("fsdp"),
        P("fsdp", None),
        P("fsdp"),
        P("fsdp", "seq", None),
    )
    out_specs = (
        P("fsdp", "seq", None),
        P("fsdp", "seq", None),
        P("fsdp"),
        P("fsdp"),
        P("fsdp", None),
        P(None, "fsdp"),
        P("fsdp", None),
        P("fsdp"),
        P("fsdp"),
        P("fsdp"),
        P("fsdp", None),
        P("fsdp"),
        P("fsdp", None),
        P("fsdp"),
    )
    return jax.shard_map(
        per_device, mesh=mesh, in_specs=in_specs, out_specs=out_specs, check_vma=False
    )
```

```python
import jax
import jax.numpy as jnp
from jax import lax
from jax.experimental import pallas as pl
from jax.experimental.pallas import tpu as pltpu
from jax.sharding import PartitionSpec as P


HEADS = 16
HEAD_DIM = 64
TILE = 256
EPSILON = 1e-05
FAR = 1e30


def gelu_tanh(values):
    return jax.nn.gelu(values, approximate=True)


def matmul(left, right):
    return jnp.dot(left, right, preferred_element_type=jnp.float32)


def left_contract(left, right):
    return lax.dot_general(
        left, right, (((0,), (0,)), ((), ())), preferred_element_type=jnp.float32
    )


def right_contract(left, right):
    return lax.dot_general(
        left, right, (((1,), (1,)), ((), ())), preferred_element_type=jnp.float32
    )


def standardize(values):
    center = values - jnp.mean(values, axis=-1, keepdims=True)
    spread = jnp.mean(center * center, axis=-1, keepdims=True)
    rate = lax.rsqrt(spread + EPSILON)
    return center * rate, rate


def norm_back(grad, gain, xhat, rate):
    e = grad * gain
    mean_e = jnp.mean(e, axis=-1, keepdims=True)
    mean_ex = jnp.mean(e * xhat, axis=-1, keepdims=True)
    return (e - mean_e - xhat * mean_ex) * rate


def half_starts(side, half):
    first = pl.multiple_of(side * half, half)
    second = pl.multiple_of(half - side * half, half)
    return first, second


def in_order(ref, first, second, half):
    return jnp.concatenate([ref[pl.ds(first, half), :], ref[pl.ds(second, half), :]], axis=0)


def tile_start(g, first, second, half):
    per_half = half // TILE
    base = first if g < per_half else second
    return pl.multiple_of(base + (g % per_half) * TILE, TILE)


def pad_head(x, a):
    zeros = jnp.zeros((HEAD_DIM, x.shape[1]), x.dtype)
    mine = x[a * HEAD_DIM : (a + 1) * HEAD_DIM]
    return jnp.concatenate([mine, zeros] if a == 0 else [zeros, mine], axis=0)


def attend_kernel(side_ref, slope_ref, q_ref, k_ref, v_ref, far_ref, out_ref, log_ref):
    length = q_ref.shape[0]
    half = length // 2
    pair = pl.program_id(0)
    first, second = half_starts(side_ref[0], half)
    keys = in_order(k_ref, first, second, half)
    values_t = in_order(v_ref, first, second, half).T
    for g in range(length // TILE):
        reach = min((g + 2) * TILE, length)
        start = tile_start(g, first, second, half)
        queries_t = (q_ref[pl.ds(start, TILE), :] * jnp.bfloat16(HEAD_DIM ** (-0.5))).T
        pieces = []
        for a in range(2):
            slope = slope_ref[2 * pair + a]
            scores = matmul(keys[:reach], pad_head(queries_t, a))
            scores = scores - slope * far_ref[:reach, g * TILE : (g + 1) * TILE]
            top = jnp.max(scores, axis=0, keepdims=True)
            weights = jnp.exp(scores - top)
            total = jnp.sum(weights, axis=0, keepdims=True)
            mixed_t = matmul(
                values_t[a * HEAD_DIM : (a + 1) * HEAD_DIM, :reach], weights.astype(jnp.bfloat16)
            )
            pieces.append(mixed_t / total)
            log_ref[0, a : a + 1, g * TILE : (g + 1) * TILE] = top + jnp.log(total)
        out_ref[pl.ds(start, TILE), :] = jnp.concatenate(pieces, axis=0).T.astype(jnp.bfloat16)


def attend_heads(joint, side, slopes, far):
    length, width = joint.shape
    pairs = width // 3 // 128
    whole = lambda offset: pl.BlockSpec((length, 128), lambda p, s: (0, p + offset))
    return pl.pallas_call(
        attend_kernel,
        grid_spec=pltpu.PrefetchScalarGridSpec(
            num_scalar_prefetch=1,
            grid=(pairs,),
            in_specs=[
                pl.BlockSpec(memory_space=pltpu.SMEM),
                whole(0),
                whole(pairs),
                whole(2 * pairs),
                pl.BlockSpec((length, length), lambda p, s: (0, 0)),
            ],
            out_specs=[
                pl.BlockSpec((length, 128), lambda p, s: (0, p)),
                pl.BlockSpec((1, 2, length), lambda p, s: (p, 0, 0)),
            ],
        ),
        out_shape=[
            jax.ShapeDtypeStruct((length, width // 3), jnp.bfloat16),
            jax.ShapeDtypeStruct((pairs, 2, length), jnp.float32),
        ],
        compiler_params=pltpu.CompilerParams(vmem_limit_bytes=48 << 20),
        name="attend",
    )(side, slopes, joint, joint, joint, far)


def back_kernel(
    side_ref,
    slope_ref,
    q_ref,
    k_ref,
    v_ref,
    far_ref,
    log_ref,
    mixed_ref,
    grad_ref,
    out_ref,
    dq_ref,
    dk_ref,
    dv_ref,
):
    length = q_ref.shape[0]
    half = length // 2
    pair = pl.program_id(0)
    part = pl.program_id(1)
    first, second = half_starts(side_ref[0], half)
    factor = HEAD_DIM ** (-0.5)

    @pl.when(part == 0)
    def _():
        keys = in_order(k_ref, first, second, half)
        keys_t = keys.T
        values = in_order(v_ref, first, second, half)
        lane = lax.broadcasted_iota(jnp.int32, (TILE, 128), 1)
        dk_ref[...] = jnp.zeros_like(dk_ref)
        dv_ref[...] = jnp.zeros_like(dv_ref)
        for g in range(length // TILE):
            reach = min((g + 2) * TILE, length)
            start = tile_start(g, first, second, half)
            queries = q_ref[pl.ds(start, TILE), :] * jnp.bfloat16(factor)
            queries_t = queries.T
            grads = grad_ref[pl.ds(start, TILE), :]
            grads_t = grads.T
            product = grads.astype(jnp.float32) * mixed_ref[pl.ds(start, TILE), :].astype(
                jnp.float32
            )
            product_t = product.T
            pieces = []
            for a in range(2):
                rows = slice(a * HEAD_DIM, (a + 1) * HEAD_DIM)
                slope = slope_ref[2 * pair + a]
                own = (lane < HEAD_DIM) if a == 0 else (lane >= HEAD_DIM)
                scores = matmul(keys[:reach], pad_head(queries_t, a))
                scores = scores - slope * far_ref[:reach, g * TILE : (g + 1) * TILE]
                probs = jnp.exp(scores - log_ref[0, a : a + 1, g * TILE : (g + 1) * TILE])
                grad_probs = matmul(values[:reach], pad_head(grads_t, a))
                inner = jnp.sum(product_t[rows], axis=0, keepdims=True)
                grad_scores = (probs * (grad_probs - inner)).astype(jnp.bfloat16)
                zero = jnp.zeros((), jnp.bfloat16)
                dk_ref[:reach] += matmul(grad_scores, jnp.where(own, queries, zero))
                dv_ref[:reach] += matmul(probs.astype(jnp.bfloat16), jnp.where(own, grads, zero))
                pieces.append(matmul(keys_t[rows, :reach], grad_scores))
            both = jnp.concatenate(pieces, axis=0).T * factor
            dq_ref[pl.ds(start, TILE), :] = both.astype(jnp.bfloat16)
        out_ref[...] = dq_ref[...]

    @pl.when(part == 1)
    def _():
        out_ref[pl.ds(first, half), :] = dk_ref[:half].astype(jnp.bfloat16)
        out_ref[pl.ds(second, half), :] = dk_ref[half:].astype(jnp.bfloat16)

    @pl.when(part == 2)
    def _():
        out_ref[pl.ds(first, half), :] = dv_ref[:half].astype(jnp.bfloat16)
        out_ref[pl.ds(second, half), :] = dv_ref[half:].astype(jnp.bfloat16)


def attend_back(joint, side, slopes, far, logs, mixed, grads):
    length, width = joint.shape
    pairs = width // 3 // 128
    whole = lambda offset: pl.BlockSpec((length, 128), lambda p, t, s: (0, p + offset))
    return pl.pallas_call(
        back_kernel,
        grid_spec=pltpu.PrefetchScalarGridSpec(
            num_scalar_prefetch=1,
            grid=(pairs, 3),
            in_specs=[
                pl.BlockSpec(memory_space=pltpu.SMEM),
                whole(0),
                whole(pairs),
                whole(2 * pairs),
                pl.BlockSpec((length, length), lambda p, t, s: (0, 0)),
                pl.BlockSpec((1, 2, length), lambda p, t, s: (p, 0, 0)),
                whole(0),
                whole(0),
            ],
            out_specs=pl.BlockSpec((length, 128), lambda p, t, s: (0, t * pairs + p)),
            scratch_shapes=[
                pltpu.VMEM((length, 128), jnp.bfloat16),
                pltpu.VMEM((length, 128), jnp.float32),
                pltpu.VMEM((length, 128), jnp.float32),
            ],
        ),
        out_shape=jax.ShapeDtypeStruct((length, width), jnp.bfloat16),
        compiler_params=pltpu.CompilerParams(vmem_limit_bytes=48 << 20),
        name="attend_back",
    )(side, slopes, joint, joint, joint, far, logs, mixed, grads)


def per_device(
    tokens,
    blocks,
    first_gain,
    first_shift,
    joint_weight,
    joint_bias,
    output_weight,
    output_bias,
    second_gain,
    second_shift,
    upward_weight,
    upward_bias,
    downward_weight,
    downward_bias,
    cotangent,
):
    groups = lax.axis_size("seq")
    shards = lax.axis_size("fsdp")
    side = lax.axis_index("seq")
    half_tokens = tokens.shape[1]
    width = tokens.shape[2]
    rows = joint_weight.shape[0]
    length = half_tokens * groups
    local_heads = HEADS // groups
    part = width // groups
    hidden_rows = downward_weight.shape[0]
    unit = hidden_rows // groups
    wide = 3 * part
    f32 = jnp.float32
    bf16 = jnp.bfloat16

    def swap(x):
        return lax.ppermute(x, "seq", [(s, groups - 1 - s) for s in range(groups)])

    def pick(x, axis, which=side):
        return lax.dynamic_index_in_dim(x, which, axis, keepdims=False)

    def gather(x):
        return lax.all_gather(x, "fsdp", axis=0, tiled=True)

    def scatter(x):
        return lax.psum_scatter(x, "fsdp", scatter_dimension=0, tiled=True)

    def weave(own, other, axis):
        return jnp.where(
            side == 0, jnp.stack([own, other], axis), jnp.stack([other, own], axis)
        )

    place = lax.axis_index("fsdp")
    bits = [1 << n for n in reversed(range((shards - 1).bit_length()))]

    def exchange(x, bit):
        return lax.ppermute(x, "fsdp", [(s, s ^ bit) for s in range(shards)])

    def tree_gather(x):
        for level, bit in enumerate(bits):
            other = exchange(x, bit)
            x = jnp.where(
                place & bit == 0,
                jnp.stack([x, other], level),
                jnp.stack([other, x], level),
            )
        return x.reshape((shards,) + x.shape[len(bits) :])

    def tree_scatter(x):
        x = x.reshape((2,) * len(bits) + x.shape[1:])
        for level, bit in reversed(list(enumerate(bits))):
            mine = (place // bit) % 2
            other = exchange(pick(x, level, 1 - mine), bit)
            x = (pick(x, level, mine).astype(f32) + other.astype(f32)).astype(x.dtype)
        return x

    token_own = tokens[0]
    grad_own = cotangent[0]
    token_other = swap(token_own)
    grad_other = swap(grad_own)

    vectors = jnp.concatenate(
        [
            first_gain,
            first_shift,
            joint_bias[0],
            joint_bias[1],
            output_bias,
            second_gain,
            second_shift,
            downward_bias,
            upward_bias,
        ]
    )
    vector_full = tree_gather(vectors[None])[:, 0].astype(f32)
    joint_part = pick(joint_weight.reshape(rows, 3, groups, part), 2).reshape(rows, wide)
    joint_full = tree_gather(joint_part).reshape(width, wide)
    up_part = pick(upward_weight.reshape(rows, shards, groups, unit), 2)
    up_part = up_part.reshape(rows, shards * unit)
    up_out_full = gather(jnp.concatenate([up_part, output_weight], axis=1))
    up_full = up_out_full[:, : shards * unit]
    out_full = up_out_full[:, shards * unit :]
    down_full = gather(pick(downward_weight.reshape(groups, unit, width), 0))

    def vector(index):
        return vector_full[:, index * rows : (index + 1) * rows].reshape(width)

    gain_one, shift_one, query_bias, value_bias = (vector(n) for n in range(4))
    out_bias, gain_two, shift_two, down_bias = (vector(n) for n in range(4, 8))
    up_bias = vector_full[:, 8 * rows : 8 * rows + hidden_rows].reshape(shards, groups, unit)
    up_bias = pick(up_bias, 1).reshape(shards * unit)
    joint_bias_part = jnp.concatenate(
        [
            pick(query_bias.reshape(groups, part), 0),
            jnp.zeros((part,), f32),
            pick(value_bias.reshape(groups, part), 0),
        ]
    )

    inputs = jnp.concatenate([token_own, token_other], axis=0).astype(f32)
    xhat_one, rate_one = standardize(inputs)
    normed_one = (xhat_one * gain_one + shift_one).astype(bf16)
    joint = (matmul(normed_one, joint_full) + joint_bias_part).astype(bf16)

    positions = jnp.arange(length)
    distance = jnp.abs(positions[:, None] - positions[None, :]).astype(f32)
    block_row = blocks[0]
    far = jnp.where(block_row[:, None] <= block_row[None, :], distance, FAR)
    head_index = side * local_heads + jnp.arange(local_heads)
    slopes = jnp.exp2(-8.0 * (head_index.astype(f32) + 1.0) / HEADS)
    side_array = side.astype(jnp.int32).reshape(1)
    mixed_own, logs = attend_heads(joint, side_array, slopes, far)

    mixed_other = swap(mixed_own)
    mixed_other = jnp.concatenate([mixed_other[half_tokens:], mixed_other[:half_tokens]], axis=0)
    mixed = jnp.concatenate([mixed_own, mixed_other], axis=1)
    out_parts = out_full.reshape(groups, part, width)
    out_turned = jnp.concatenate([pick(out_parts, 0), pick(out_parts, 0, groups - 1 - side)], axis=0)
    hidden = inputs + matmul(mixed, out_turned) + out_bias
    xhat_two, rate_two = standardize(hidden)
    normed_two = (xhat_two * gain_two + shift_two).astype(bf16)
    upward = matmul(normed_two, up_full) + up_bias
    activated = gelu_tanh(upward).astype(bf16)

    grad_low = jnp.concatenate([grad_own, grad_other], axis=0)
    grad_down = left_contract(activated, grad_low).astype(bf16)
    down_full, grad_down = lax.optimization_barrier((down_full, grad_down))
    grad_down = scatter(grad_down)
    grad_act = right_contract(grad_low, down_full)
    grad_up = jax.vjp(gelu_tanh, upward)[1](grad_act)[0].astype(bf16)
    grad_two = right_contract(grad_up, up_full)
    grad_two_other = swap(grad_two[half_tokens:].astype(bf16))
    grad_up_weight = left_contract(normed_two, grad_up).astype(bf16)
    grad_two_other, grad_up_weight = lax.optimization_barrier((grad_two_other, grad_up_weight))
    grad_up_weight = scatter(grad_up_weight)
    grad_two_own = grad_two[:half_tokens] + grad_two_other.astype(f32)
    grad_hidden = grad_own.astype(f32) + norm_back(
        grad_two_own, gain_two, xhat_two[:half_tokens], rate_two[:half_tokens]
    )
    hidden_low = grad_hidden.astype(bf16)

    grad_mixed = right_contract(hidden_low, out_turned).astype(bf16)
    grad_heads_other = swap(grad_mixed[:, part:])
    late_activated, grad_mixed = lax.optimization_barrier((activated, grad_mixed))
    partial_out = matmul(late_activated, down_full)
    partial_own = partial_out[:half_tokens]
    partial_other = partial_out[half_tokens:].astype(bf16)
    grad_heads_other, partial_other = lax.optimization_barrier((grad_heads_other, partial_other))
    result_other = swap(partial_other)
    grad_heads = jnp.concatenate([grad_mixed[:, :part], grad_heads_other], axis=0)
    grad_joint = attend_back(joint, side_array, slopes, far, logs, mixed_own, grad_heads)

    low_parts = hidden_low.reshape(half_tokens, groups, part)
    low_columns = jnp.concatenate(
        [pick(low_parts, 1), swap(pick(low_parts, 1, groups - 1 - side))], axis=0
    )
    grad_out = left_contract(mixed, low_columns).astype(bf16)
    out_rows = grad_out.reshape(groups, part, part)
    grad_out = jnp.concatenate([pick(out_rows, 0), pick(out_rows, 0, groups - 1 - side)], axis=0)

    result = hidden[:half_tokens] + partial_own + result_other.astype(f32) + down_bias

    grad_joint_weight = left_contract(normed_one, grad_joint).astype(bf16)
    last = jnp.concatenate([grad_joint_weight, grad_out], axis=1)
    last = last.reshape(shards, rows, wide + part)
    grad_joint, last = lax.optimization_barrier((grad_joint, last))
    last = tree_scatter(last)
    grad_one = right_contract(grad_joint, joint_full)

    def spread(x):
        empty = jnp.zeros_like(x)
        return weave(x, empty, 0).reshape(width)

    joint_sums = jnp.sum(grad_joint.astype(f32), axis=0)
    sums = [
        jnp.sum(grad_one * xhat_one, axis=0),
        jnp.sum(grad_one, axis=0),
        spread(joint_sums[:part]),
        spread(joint_sums[2 * part :]),
        jnp.sum(hidden_low.astype(f32), axis=0),
        jnp.sum(grad_two * xhat_two, axis=0),
        jnp.sum(grad_two, axis=0),
        jnp.sum(grad_own.astype(f32), axis=0),
    ]
    up_sums = jnp.sum(grad_up.astype(f32), axis=0).reshape(shards, unit)
    up_sums = weave(up_sums, jnp.zeros_like(up_sums), 1).reshape(shards, hidden_rows)
    sum_rows = jnp.concatenate([s.reshape(shards, rows) for s in sums] + [up_sums], axis=1)
    vector_total = tree_scatter(sum_rows[:, None])[0]
    vector_total = vector_total + swap(vector_total)

    grad_one_own = grad_one[:half_tokens] + swap(grad_one[half_tokens:].astype(bf16)).astype(f32)
    grad_tokens = grad_hidden + norm_back(
        grad_one_own, gain_one, xhat_one[:half_tokens], rate_one[:half_tokens]
    )

    down_total = weave(grad_down, swap(grad_down), 0).reshape(hidden_rows, width)
    up_own = grad_up_weight.reshape(rows, shards, unit)
    up_other = swap(grad_up_weight).reshape(rows, shards, unit)
    up_total = weave(up_own, up_other, 2).reshape(rows, shards * hidden_rows)
    last_other = swap(last)
    joint_total = weave(
        last[:, :wide].reshape(rows, 3, part), last_other[:, :wide].reshape(rows, 3, part), 2
    ).reshape(rows, 3 * width)
    out_total = weave(last[:, wide:], last_other[:, wide:], 1).reshape(rows, width)

    def total(index):
        return vector_total[index * rows : (index + 1) * rows]

    return (
        result.astype(bf16)[None],
        grad_tokens[None],
        total(0),
        total(1),
        joint_total.astype(f32),
        jnp.stack([total(2), total(3)]),
        out_total.astype(f32),
        total(4),
        total(5),
        total(6),
        up_total.astype(f32),
        vector_total[8 * rows : 8 * rows + hidden_rows],
        down_total.astype(f32),
        total(7),
    )


def solution(mesh):
    in_specs = (
        P("fsdp", "seq", None),
        P("fsdp", None),
        P("fsdp"),
        P("fsdp"),
        P("fsdp", None),
        P(None, "fsdp"),
        P("fsdp", None),
        P("fsdp"),
        P("fsdp"),
        P("fsdp"),
        P("fsdp", None),
        P("fsdp"),
        P("fsdp", None),
        P("fsdp"),
        P("fsdp", "seq", None),
    )
    out_specs = (
        P("fsdp", "seq", None),
        P("fsdp", "seq", None),
        P("fsdp"),
        P("fsdp"),
        P("fsdp", None),
        P(None, "fsdp"),
        P("fsdp", None),
        P("fsdp"),
        P("fsdp"),
        P("fsdp"),
        P("fsdp", None),
        P("fsdp"),
        P("fsdp", None),
        P("fsdp"),
    )
    return jax.shard_map(
        per_device, mesh=mesh, in_specs=in_specs, out_specs=out_specs, check_vma=False
    )
```

```python
import functools

import jax
import jax.numpy as jnp
from jax import lax
from jax.experimental import pallas as pl
from jax.experimental.pallas import tpu as pltpu
from jax.sharding import PartitionSpec as P


HEADS = 16
HEAD_DIM = 64
TILE = 256
EPSILON = 1e-05
FAR = 1e30


def gelu_tanh(values):
    return jax.nn.gelu(values, approximate=True)


def matmul(left, right):
    return jnp.dot(left, right, preferred_element_type=jnp.float32)


def left_contract(left, right):
    return lax.dot_general(
        left, right, (((0,), (0,)), ((), ())), preferred_element_type=jnp.float32
    )


def right_contract(left, right):
    return lax.dot_general(
        left, right, (((1,), (1,)), ((), ())), preferred_element_type=jnp.float32
    )


def standardize(values):
    center = values - jnp.mean(values, axis=-1, keepdims=True)
    spread = jnp.mean(center * center, axis=-1, keepdims=True)
    rate = lax.rsqrt(spread + EPSILON)
    return center * rate, rate


def norm_back(grad, gain, xhat, rate):
    e = grad * gain
    mean_e = jnp.mean(e, axis=-1, keepdims=True)
    mean_ex = jnp.mean(e * xhat, axis=-1, keepdims=True)
    return (e - mean_e - xhat * mean_ex) * rate


def half_starts(side, half):
    first = pl.multiple_of(side * half, half)
    second = pl.multiple_of(half - side * half, half)
    return first, second


def in_order(ref, first, second, half):
    return jnp.concatenate([ref[pl.ds(first, half), :], ref[pl.ds(second, half), :]], axis=0)


def tile_start(g, first, second, half):
    per_half = half // TILE
    base = first if g < per_half else second
    return pl.multiple_of(base + (g % per_half) * TILE, TILE)


def pad_head(x, a):
    zeros = jnp.zeros((HEAD_DIM, x.shape[1]), x.dtype)
    mine = x[a * HEAD_DIM : (a + 1) * HEAD_DIM]
    return jnp.concatenate([mine, zeros] if a == 0 else [zeros, mine], axis=0)


def attend_kernel(begin, side_ref, slope_ref, q_ref, k_ref, v_ref, far_ref, out_ref, log_ref):
    length = q_ref.shape[0]
    half = length // 2
    pair = pl.program_id(0) + begin
    first, second = half_starts(side_ref[0], half)
    keys = in_order(k_ref, first, second, half)
    values_t = in_order(v_ref, first, second, half).T
    for g in range(length // TILE):
        reach = min((g + 2) * TILE, length)
        start = tile_start(g, first, second, half)
        queries_t = (q_ref[pl.ds(start, TILE), :] * jnp.bfloat16(HEAD_DIM ** (-0.5))).T
        pieces = []
        for a in range(2):
            slope = slope_ref[2 * pair + a]
            scores = matmul(keys[:reach], pad_head(queries_t, a))
            scores = scores - slope * far_ref[:reach, g * TILE : (g + 1) * TILE]
            top = jnp.max(scores, axis=0, keepdims=True)
            weights = jnp.exp(scores - top)
            total = jnp.sum(weights, axis=0, keepdims=True)
            mixed_t = matmul(
                values_t[a * HEAD_DIM : (a + 1) * HEAD_DIM, :reach], weights.astype(jnp.bfloat16)
            )
            pieces.append(mixed_t / total)
            log_ref[0, a : a + 1, g * TILE : (g + 1) * TILE] = top + jnp.log(total)
        out_ref[pl.ds(start, TILE), :] = jnp.concatenate(pieces, axis=0).T.astype(jnp.bfloat16)


def attend_heads(joint, side, slopes, far, begin, count):
    length, width = joint.shape
    pairs = width // 3 // 128
    whole = lambda offset: pl.BlockSpec((length, 128), lambda p, s: (0, p + offset))
    return pl.pallas_call(
        functools.partial(attend_kernel, begin),
        grid_spec=pltpu.PrefetchScalarGridSpec(
            num_scalar_prefetch=1,
            grid=(count,),
            in_specs=[
                pl.BlockSpec(memory_space=pltpu.SMEM),
                whole(begin),
                whole(begin + pairs),
                whole(begin + 2 * pairs),
                pl.BlockSpec((length, length), lambda p, s: (0, 0)),
            ],
            out_specs=[
                pl.BlockSpec((length, 128), lambda p, s: (0, p)),
                pl.BlockSpec((1, 2, length), lambda p, s: (p, 0, 0)),
            ],
        ),
        out_shape=[
            jax.ShapeDtypeStruct((length, count * 128), jnp.bfloat16),
            jax.ShapeDtypeStruct((count, 2, length), jnp.float32),
        ],
        compiler_params=pltpu.CompilerParams(vmem_limit_bytes=48 << 20),
        name="attend",
    )(side, slopes, joint, joint, joint, far)


def back_kernel(
    side_ref,
    slope_ref,
    q_ref,
    k_ref,
    v_ref,
    far_ref,
    log_ref,
    mixed_ref,
    grad_ref,
    out_ref,
    dq_ref,
    dk_ref,
    dv_ref,
):
    length = q_ref.shape[0]
    half = length // 2
    pair = pl.program_id(0)
    part = pl.program_id(1)
    first, second = half_starts(side_ref[0], half)
    factor = HEAD_DIM ** (-0.5)

    @pl.when(part == 0)
    def _():
        keys = in_order(k_ref, first, second, half)
        keys_t = keys.T
        values = in_order(v_ref, first, second, half)
        lane = lax.broadcasted_iota(jnp.int32, (TILE, 128), 1)
        dk_ref[...] = jnp.zeros_like(dk_ref)
        dv_ref[...] = jnp.zeros_like(dv_ref)
        for g in range(length // TILE):
            reach = min((g + 2) * TILE, length)
            start = tile_start(g, first, second, half)
            queries = q_ref[pl.ds(start, TILE), :] * jnp.bfloat16(factor)
            queries_t = queries.T
            grads = grad_ref[pl.ds(start, TILE), :]
            grads_t = grads.T
            product = grads.astype(jnp.float32) * mixed_ref[pl.ds(start, TILE), :].astype(
                jnp.float32
            )
            product_t = product.T
            pieces = []
            for a in range(2):
                rows = slice(a * HEAD_DIM, (a + 1) * HEAD_DIM)
                slope = slope_ref[2 * pair + a]
                own = (lane < HEAD_DIM) if a == 0 else (lane >= HEAD_DIM)
                scores = matmul(keys[:reach], pad_head(queries_t, a))
                scores = scores - slope * far_ref[:reach, g * TILE : (g + 1) * TILE]
                probs = jnp.exp(scores - log_ref[0, a : a + 1, g * TILE : (g + 1) * TILE])
                grad_probs = matmul(values[:reach], pad_head(grads_t, a))
                inner = jnp.sum(product_t[rows], axis=0, keepdims=True)
                grad_scores = (probs * (grad_probs - inner)).astype(jnp.bfloat16)
                zero = jnp.zeros((), jnp.bfloat16)
                dk_ref[:reach] += matmul(grad_scores, jnp.where(own, queries, zero))
                dv_ref[:reach] += matmul(probs.astype(jnp.bfloat16), jnp.where(own, grads, zero))
                pieces.append(matmul(keys_t[rows, :reach], grad_scores))
            both = jnp.concatenate(pieces, axis=0).T * factor
            dq_ref[pl.ds(start, TILE), :] = both.astype(jnp.bfloat16)
        out_ref[...] = dq_ref[...]

    @pl.when(part == 1)
    def _():
        out_ref[pl.ds(first, half), :] = dk_ref[:half].astype(jnp.bfloat16)
        out_ref[pl.ds(second, half), :] = dk_ref[half:].astype(jnp.bfloat16)

    @pl.when(part == 2)
    def _():
        out_ref[pl.ds(first, half), :] = dv_ref[:half].astype(jnp.bfloat16)
        out_ref[pl.ds(second, half), :] = dv_ref[half:].astype(jnp.bfloat16)


def attend_back(joint, side, slopes, far, logs, mixed, grads):
    length, width = joint.shape
    pairs = width // 3 // 128
    whole = lambda offset: pl.BlockSpec((length, 128), lambda p, t, s: (0, p + offset))
    return pl.pallas_call(
        back_kernel,
        grid_spec=pltpu.PrefetchScalarGridSpec(
            num_scalar_prefetch=1,
            grid=(pairs, 3),
            in_specs=[
                pl.BlockSpec(memory_space=pltpu.SMEM),
                whole(0),
                whole(pairs),
                whole(2 * pairs),
                pl.BlockSpec((length, length), lambda p, t, s: (0, 0)),
                pl.BlockSpec((1, 2, length), lambda p, t, s: (p, 0, 0)),
                whole(0),
                whole(0),
            ],
            out_specs=pl.BlockSpec((length, 128), lambda p, t, s: (0, t * pairs + p)),
            scratch_shapes=[
                pltpu.VMEM((length, 128), jnp.bfloat16),
                pltpu.VMEM((length, 128), jnp.float32),
                pltpu.VMEM((length, 128), jnp.float32),
            ],
        ),
        out_shape=jax.ShapeDtypeStruct((length, width), jnp.bfloat16),
        compiler_params=pltpu.CompilerParams(vmem_limit_bytes=48 << 20),
        name="attend_back",
    )(side, slopes, joint, joint, joint, far, logs, mixed, grads)


def per_device(
    tokens,
    blocks,
    first_gain,
    first_shift,
    joint_weight,
    joint_bias,
    output_weight,
    output_bias,
    second_gain,
    second_shift,
    upward_weight,
    upward_bias,
    downward_weight,
    downward_bias,
    cotangent,
):
    groups = lax.axis_size("seq")
    shards = lax.axis_size("fsdp")
    side = lax.axis_index("seq")
    half_tokens = tokens.shape[1]
    width = tokens.shape[2]
    rows = joint_weight.shape[0]
    length = half_tokens * groups
    local_heads = HEADS // groups
    part = width // groups
    hidden_rows = downward_weight.shape[0]
    unit = hidden_rows // groups
    wide = 3 * part
    f32 = jnp.float32
    bf16 = jnp.bfloat16

    def swap(x):
        return lax.ppermute(x, "seq", [(s, groups - 1 - s) for s in range(groups)])

    def pick(x, axis, which=side):
        return lax.dynamic_index_in_dim(x, which, axis, keepdims=False)

    def gather(x):
        return lax.all_gather(x, "fsdp", axis=0, tiled=True)

    def scatter(x):
        return lax.psum_scatter(x, "fsdp", scatter_dimension=0, tiled=True)

    def weave(own, other, axis):
        return jnp.where(
            side == 0, jnp.stack([own, other], axis), jnp.stack([other, own], axis)
        )

    place = lax.axis_index("fsdp")
    bits = [1 << n for n in reversed(range((shards - 1).bit_length()))]

    def exchange(x, bit):
        return lax.ppermute(x, "fsdp", [(s, s ^ bit) for s in range(shards)])

    def tree_gather(x):
        for level, bit in enumerate(bits):
            other = exchange(x, bit)
            x = jnp.where(
                place & bit == 0,
                jnp.stack([x, other], level),
                jnp.stack([other, x], level),
            )
        return x.reshape((shards,) + x.shape[len(bits) :])

    def tree_step(x, level):
        mine = (place // bits[level]) % 2
        other = exchange(pick(x, level, 1 - mine), bits[level])
        return (pick(x, level, mine).astype(f32) + other.astype(f32)).astype(x.dtype)

    def tree_shape(x):
        return x.reshape((2,) * len(bits) + x.shape[1:])

    def tree_scatter(x):
        x = tree_shape(x)
        for level in reversed(range(len(bits))):
            x = tree_step(x, level)
        return x

    token_own = tokens[0]
    grad_own = cotangent[0]
    token_other = swap(token_own)
    grad_other = swap(grad_own)

    vectors = jnp.concatenate(
        [
            first_gain,
            first_shift,
            joint_bias[0],
            joint_bias[1],
            output_bias,
            second_gain,
            second_shift,
            downward_bias,
            upward_bias,
        ]
    )
    vector_full = tree_gather(vectors[None])[:, 0].astype(f32)
    joint_part = pick(joint_weight.reshape(rows, 3, groups, part), 2).reshape(rows, wide)
    joint_full = gather(joint_part)
    up_part = pick(upward_weight.reshape(rows, shards, groups, unit), 2)
    up_part = up_part.reshape(rows, shards * unit)
    up_out_full = gather(jnp.concatenate([up_part, output_weight], axis=1))
    up_full = up_out_full[:, : shards * unit]
    out_full = up_out_full[:, shards * unit :]
    down_part = pick(downward_weight.reshape(groups, unit, width), 0)
    down_full = tree_gather(down_part).reshape(shards * unit, width)

    def vector(index):
        return vector_full[:, index * rows : (index + 1) * rows].reshape(width)

    gain_one, shift_one, query_bias, value_bias = (vector(n) for n in range(4))
    out_bias, gain_two, shift_two, down_bias = (vector(n) for n in range(4, 8))
    up_bias = vector_full[:, 8 * rows : 8 * rows + hidden_rows].reshape(shards, groups, unit)
    up_bias = pick(up_bias, 1).reshape(shards * unit)
    joint_bias_part = jnp.concatenate(
        [
            pick(query_bias.reshape(groups, part), 0),
            jnp.zeros((part,), f32),
            pick(value_bias.reshape(groups, part), 0),
        ]
    )

    inputs = jnp.concatenate([token_own, token_other], axis=0).astype(f32)
    xhat_one, rate_one = standardize(inputs)
    normed_one = (xhat_one * gain_one + shift_one).astype(bf16)
    joint = (matmul(normed_one, joint_full) + joint_bias_part).astype(bf16)

    positions = jnp.arange(length)
    distance = jnp.abs(positions[:, None] - positions[None, :]).astype(f32)
    block_row = blocks[0]
    far = jnp.where(block_row[:, None] <= block_row[None, :], distance, FAR)
    head_index = side * local_heads + jnp.arange(local_heads)
    slopes = jnp.exp2(-8.0 * (head_index.astype(f32) + 1.0) / HEADS)
    side_array = side.astype(jnp.int32).reshape(1)
    pairs = part // 128
    calls = 2
    chunk = pairs // calls
    own_parts, other_parts, log_parts = [], [], []
    for call in range(calls):
        mixed_part, log_part = attend_heads(
            joint, side_array, slopes, far, call * chunk, chunk
        )
        other = swap(mixed_part)
        own_parts.append(mixed_part)
        log_parts.append(log_part)
        other_parts.append(jnp.concatenate([other[half_tokens:], other[:half_tokens]], axis=0))
    logs = jnp.concatenate(log_parts, axis=0)
    mixed_own = jnp.concatenate(own_parts, axis=1)
    mixed = jnp.where(
        side == 0,
        jnp.concatenate(own_parts + other_parts, axis=1),
        jnp.concatenate(other_parts + own_parts, axis=1),
    )
    hidden = inputs + matmul(mixed, out_full) + out_bias
    xhat_two, rate_two = standardize(hidden)
    normed_two = (xhat_two * gain_two + shift_two).astype(bf16)
    upward = matmul(normed_two, up_full) + up_bias
    activated = gelu_tanh(upward).astype(bf16)

    grad_low = jnp.concatenate([grad_own, grad_other], axis=0)
    grad_down = left_contract(activated, grad_low).astype(bf16)
    down_full, grad_down = lax.optimization_barrier((down_full, grad_down))
    grad_down = scatter(grad_down)

    def feed_back(grad, before):
        grad_act = right_contract(grad, down_full)
        grad_up = jax.vjp(gelu_tanh, before)[1](grad_act)[0].astype(bf16)
        return grad_up, right_contract(grad_up, up_full)

    grad_up_far, grad_two_far = feed_back(grad_other, upward[half_tokens:])
    grad_two_low, grad_near = lax.optimization_barrier((grad_two_far.astype(bf16), grad_own))
    grad_two_other = swap(grad_two_low)
    grad_up_near, grad_two_near = feed_back(grad_near, upward[:half_tokens])
    grad_up = jnp.concatenate([grad_up_near, grad_up_far], axis=0)
    grad_up_weight = left_contract(normed_two, grad_up).astype(bf16)
    grad_two_other, grad_up_weight = lax.optimization_barrier((grad_two_other, grad_up_weight))
    grad_up_weight = scatter(grad_up_weight)
    grad_two_own = grad_two_near + grad_two_other.astype(f32)
    grad_hidden = grad_own.astype(f32) + norm_back(
        grad_two_own, gain_two, xhat_two[:half_tokens], rate_two[:half_tokens]
    )
    hidden_low = grad_hidden.astype(bf16)

    grad_mixed = right_contract(hidden_low, out_full).astype(bf16)
    mixed_parts = grad_mixed.reshape(half_tokens, groups, part)
    grad_heads_other = swap(pick(mixed_parts, 1, groups - 1 - side))
    late_activated, mixed_parts = lax.optimization_barrier((activated, mixed_parts))
    partial_out = matmul(late_activated, down_full)
    partial_own = partial_out[:half_tokens]
    partial_other = partial_out[half_tokens:].astype(bf16)
    grad_heads_other, partial_other, hidden_late = lax.optimization_barrier(
        (grad_heads_other, partial_other, hidden_low)
    )
    low_parts = hidden_late.reshape(half_tokens, groups, part)
    low_other = swap(pick(low_parts, 1, groups - 1 - side))
    result_other = swap(partial_other)
    grad_heads = jnp.concatenate([pick(mixed_parts, 1), grad_heads_other], axis=0)
    grad_joint = attend_back(joint, side_array, slopes, far, logs, mixed_own, grad_heads)
    grad_joint, low_other = lax.optimization_barrier((grad_joint, low_other))

    low_columns = jnp.concatenate([pick(low_parts, 1), low_other], axis=0)
    grad_out = left_contract(mixed, low_columns).astype(bf16)
    result = hidden[:half_tokens] + partial_own + result_other.astype(f32) + down_bias

    grad_joint_weight = left_contract(normed_one, grad_joint).astype(bf16)
    last = jnp.concatenate([grad_joint_weight, grad_out], axis=1)
    last = last.reshape(shards, rows, wide + part)
    grad_joint, last, grad_down = lax.optimization_barrier((grad_joint, last, grad_down))
    last = tree_step(tree_shape(last), len(bits) - 1)
    grad_one_far = right_contract(grad_joint[half_tokens:], joint_full)
    grad_one_other = swap(grad_one_far.astype(bf16))
    grad_one_near = right_contract(grad_joint[:half_tokens], joint_full)
    last, grad_one_other = lax.optimization_barrier((last, grad_one_other))
    last = tree_step(last, len(bits) - 2)

    def spread(x):
        empty = jnp.zeros_like(x)
        return weave(x, empty, 0).reshape(width)

    joint_sums = jnp.sum(grad_joint.astype(f32), axis=0)
    sums = [
        jnp.sum(grad_one_near * xhat_one[:half_tokens], axis=0)
        + jnp.sum(grad_one_far * xhat_one[half_tokens:], axis=0),
        jnp.sum(grad_one_near, axis=0) + jnp.sum(grad_one_far, axis=0),
        spread(joint_sums[:part]),
        spread(joint_sums[2 * part :]),
        jnp.sum(hidden_low.astype(f32), axis=0),
        jnp.sum(grad_two_near * xhat_two[:half_tokens], axis=0)
        + jnp.sum(grad_two_far * xhat_two[half_tokens:], axis=0),
        jnp.sum(grad_two_near, axis=0) + jnp.sum(grad_two_far, axis=0),
        jnp.sum(grad_own.astype(f32), axis=0),
    ]
    up_sums = jnp.sum(grad_up.astype(f32), axis=0).reshape(shards, unit)
    up_sums = weave(up_sums, jnp.zeros_like(up_sums), 1).reshape(shards, hidden_rows)
    sum_rows = jnp.concatenate([s.reshape(shards, rows) for s in sums] + [up_sums], axis=1)
    last, sum_rows = lax.optimization_barrier((last, sum_rows))
    for level in reversed(range(len(bits) - 2)):
        last = tree_step(last, level)
    vector_total = tree_scatter(sum_rows[:, None])[0]
    vector_total = vector_total + swap(vector_total)

    grad_one_own = grad_one_near + grad_one_other.astype(f32)
    grad_tokens = grad_hidden + norm_back(
        grad_one_own, gain_one, xhat_one[:half_tokens], rate_one[:half_tokens]
    )

    down_total = weave(grad_down, swap(grad_down), 0).reshape(hidden_rows, width)
    up_own = grad_up_weight.reshape(rows, shards, unit)
    up_other = swap(grad_up_weight).reshape(rows, shards, unit)
    up_total = weave(up_own, up_other, 2).reshape(rows, shards * hidden_rows)
    last_other = swap(last)
    joint_total = weave(
        last[:, :wide].reshape(rows, 3, part), last_other[:, :wide].reshape(rows, 3, part), 2
    ).reshape(rows, 3 * width)
    out_total = weave(last[:, wide:], last_other[:, wide:], 1).reshape(rows, width)

    def total(index):
        return vector_total[index * rows : (index + 1) * rows]

    return (
        result.astype(bf16)[None],
        grad_tokens[None],
        total(0),
        total(1),
        joint_total.astype(f32),
        jnp.stack([total(2), total(3)]),
        out_total.astype(f32),
        total(4),
        total(5),
        total(6),
        up_total.astype(f32),
        vector_total[8 * rows : 8 * rows + hidden_rows],
        down_total.astype(f32),
        total(7),
    )


def solution(mesh):
    in_specs = (
        P("fsdp", "seq", None),
        P("fsdp", None),
        P("fsdp"),
        P("fsdp"),
        P("fsdp", None),
        P(None, "fsdp"),
        P("fsdp", None),
        P("fsdp"),
        P("fsdp"),
        P("fsdp"),
        P("fsdp", None),
        P("fsdp"),
        P("fsdp", None),
        P("fsdp"),
        P("fsdp", "seq", None),
    )
    out_specs = (
        P("fsdp", "seq", None),
        P("fsdp", "seq", None),
        P("fsdp"),
        P("fsdp"),
        P("fsdp", None),
        P(None, "fsdp"),
        P("fsdp", None),
        P("fsdp"),
        P("fsdp"),
        P("fsdp"),
        P("fsdp", None),
        P("fsdp"),
        P("fsdp", None),
        P("fsdp"),
    )
    return jax.shard_map(
        per_device, mesh=mesh, in_specs=in_specs, out_specs=out_specs, check_vma=False
    )
```

```python
import functools

import jax
import jax.numpy as jnp
from jax import lax
from jax.experimental import pallas as pl
from jax.experimental.pallas import tpu as pltpu
from jax.sharding import PartitionSpec as P


HEADS = 16
HEAD_DIM = 64
TILE = 256
EPSILON = 1e-05
FAR = 1e30


def gelu_tanh(values):
    return jax.nn.gelu(values, approximate=True)


def matmul(left, right):
    return jnp.dot(left, right, preferred_element_type=jnp.float32)


def left_contract(left, right):
    return lax.dot_general(
        left, right, (((0,), (0,)), ((), ())), preferred_element_type=jnp.float32
    )


def right_contract(left, right):
    return lax.dot_general(
        left, right, (((1,), (1,)), ((), ())), preferred_element_type=jnp.float32
    )


def standardize(values):
    center = values - jnp.mean(values, axis=-1, keepdims=True)
    spread = jnp.mean(center * center, axis=-1, keepdims=True)
    rate = lax.rsqrt(spread + EPSILON)
    return center * rate, rate


def norm_back(grad, gain, xhat, rate):
    e = grad * gain
    mean_e = jnp.mean(e, axis=-1, keepdims=True)
    mean_ex = jnp.mean(e * xhat, axis=-1, keepdims=True)
    return (e - mean_e - xhat * mean_ex) * rate


def half_starts(side, half):
    first = pl.multiple_of(side * half, half)
    second = pl.multiple_of(half - side * half, half)
    return first, second


def in_order(ref, first, second, half):
    return jnp.concatenate([ref[pl.ds(first, half), :], ref[pl.ds(second, half), :]], axis=0)


def tile_start(g, first, second, half):
    per_half = half // TILE
    base = first if g < per_half else second
    return pl.multiple_of(base + (g % per_half) * TILE, TILE)


def pad_head(x, a):
    zeros = jnp.zeros((HEAD_DIM, x.shape[1]), x.dtype)
    mine = x[a * HEAD_DIM : (a + 1) * HEAD_DIM]
    return jnp.concatenate([mine, zeros] if a == 0 else [zeros, mine], axis=0)


def attend_kernel(begin, side_ref, slope_ref, q_ref, k_ref, v_ref, far_ref, out_ref, log_ref):
    length = q_ref.shape[0]
    half = length // 2
    pair = pl.program_id(0) + begin
    first, second = half_starts(side_ref[0], half)
    keys = in_order(k_ref, first, second, half)
    values_t = in_order(v_ref, first, second, half).T
    for g in range(length // TILE):
        reach = min((g + 2) * TILE, length)
        start = tile_start(g, first, second, half)
        queries_t = (q_ref[pl.ds(start, TILE), :] * jnp.bfloat16(HEAD_DIM ** (-0.5))).T
        pieces = []
        for a in range(2):
            slope = slope_ref[2 * pair + a]
            scores = matmul(keys[:reach], pad_head(queries_t, a))
            scores = scores - slope * far_ref[:reach, g * TILE : (g + 1) * TILE]
            top = jnp.max(scores, axis=0, keepdims=True)
            weights = jnp.exp(scores - top)
            total = jnp.sum(weights, axis=0, keepdims=True)
            mixed_t = matmul(
                values_t[a * HEAD_DIM : (a + 1) * HEAD_DIM, :reach], weights.astype(jnp.bfloat16)
            )
            pieces.append(mixed_t / total)
            log_ref[0, a : a + 1, g * TILE : (g + 1) * TILE] = top + jnp.log(total)
        out_ref[pl.ds(start, TILE), :] = jnp.concatenate(pieces, axis=0).T.astype(jnp.bfloat16)


def attend_heads(joint, side, slopes, far, begin, count):
    length, width = joint.shape
    pairs = width // 3 // 128
    whole = lambda offset: pl.BlockSpec((length, 128), lambda p, s: (0, p + offset))
    return pl.pallas_call(
        functools.partial(attend_kernel, begin),
        grid_spec=pltpu.PrefetchScalarGridSpec(
            num_scalar_prefetch=1,
            grid=(count,),
            in_specs=[
                pl.BlockSpec(memory_space=pltpu.SMEM),
                whole(begin),
                whole(begin + pairs),
                whole(begin + 2 * pairs),
                pl.BlockSpec((length, length), lambda p, s: (0, 0)),
            ],
            out_specs=[
                pl.BlockSpec((length, 128), lambda p, s: (0, p)),
                pl.BlockSpec((1, 2, length), lambda p, s: (p, 0, 0)),
            ],
        ),
        out_shape=[
            jax.ShapeDtypeStruct((length, count * 128), jnp.bfloat16),
            jax.ShapeDtypeStruct((count, 2, length), jnp.float32),
        ],
        compiler_params=pltpu.CompilerParams(vmem_limit_bytes=48 << 20),
        name="attend",
    )(side, slopes, joint, joint, joint, far)


def back_kernel(
    side_ref,
    slope_ref,
    q_ref,
    k_ref,
    v_ref,
    far_ref,
    log_ref,
    mixed_ref,
    grad_ref,
    out_ref,
    dq_ref,
    dk_ref,
    dv_ref,
):
    length = q_ref.shape[0]
    half = length // 2
    pair = pl.program_id(0)
    part = pl.program_id(1)
    first, second = half_starts(side_ref[0], half)
    factor = HEAD_DIM ** (-0.5)

    @pl.when(part == 0)
    def _():
        keys = in_order(k_ref, first, second, half)
        keys_t = keys.T
        values = in_order(v_ref, first, second, half)
        lane = lax.broadcasted_iota(jnp.int32, (TILE, 128), 1)
        dk_ref[...] = jnp.zeros_like(dk_ref)
        dv_ref[...] = jnp.zeros_like(dv_ref)
        for g in range(length // TILE):
            reach = min((g + 2) * TILE, length)
            start = tile_start(g, first, second, half)
            queries = q_ref[pl.ds(start, TILE), :] * jnp.bfloat16(factor)
            queries_t = queries.T
            grads = grad_ref[pl.ds(start, TILE), :]
            grads_t = grads.T
            product = grads.astype(jnp.float32) * mixed_ref[pl.ds(start, TILE), :].astype(
                jnp.float32
            )
            product_t = product.T
            pieces = []
            for a in range(2):
                rows = slice(a * HEAD_DIM, (a + 1) * HEAD_DIM)
                slope = slope_ref[2 * pair + a]
                own = (lane < HEAD_DIM) if a == 0 else (lane >= HEAD_DIM)
                scores = matmul(keys[:reach], pad_head(queries_t, a))
                scores = scores - slope * far_ref[:reach, g * TILE : (g + 1) * TILE]
                probs = jnp.exp(scores - log_ref[0, a : a + 1, g * TILE : (g + 1) * TILE])
                grad_probs = matmul(values[:reach], pad_head(grads_t, a))
                inner = jnp.sum(product_t[rows], axis=0, keepdims=True)
                grad_scores = (probs * (grad_probs - inner)).astype(jnp.bfloat16)
                zero = jnp.zeros((), jnp.bfloat16)
                dk_ref[:reach] += matmul(grad_scores, jnp.where(own, queries, zero))
                dv_ref[:reach] += matmul(probs.astype(jnp.bfloat16), jnp.where(own, grads, zero))
                pieces.append(matmul(keys_t[rows, :reach], grad_scores))
            both = jnp.concatenate(pieces, axis=0).T * factor
            dq_ref[pl.ds(start, TILE), :] = both.astype(jnp.bfloat16)
        out_ref[...] = dq_ref[...]

    @pl.when(part == 1)
    def _():
        out_ref[pl.ds(first, half), :] = dk_ref[:half].astype(jnp.bfloat16)
        out_ref[pl.ds(second, half), :] = dk_ref[half:].astype(jnp.bfloat16)

    @pl.when(part == 2)
    def _():
        out_ref[pl.ds(first, half), :] = dv_ref[:half].astype(jnp.bfloat16)
        out_ref[pl.ds(second, half), :] = dv_ref[half:].astype(jnp.bfloat16)


def attend_back(joint, side, slopes, far, logs, mixed, grads):
    length, width = joint.shape
    pairs = width // 3 // 128
    whole = lambda offset: pl.BlockSpec((length, 128), lambda p, t, s: (0, p + offset))
    return pl.pallas_call(
        back_kernel,
        grid_spec=pltpu.PrefetchScalarGridSpec(
            num_scalar_prefetch=1,
            grid=(pairs, 3),
            in_specs=[
                pl.BlockSpec(memory_space=pltpu.SMEM),
                whole(0),
                whole(pairs),
                whole(2 * pairs),
                pl.BlockSpec((length, length), lambda p, t, s: (0, 0)),
                pl.BlockSpec((1, 2, length), lambda p, t, s: (p, 0, 0)),
                whole(0),
                whole(0),
            ],
            out_specs=pl.BlockSpec((length, 128), lambda p, t, s: (0, t * pairs + p)),
            scratch_shapes=[
                pltpu.VMEM((length, 128), jnp.bfloat16),
                pltpu.VMEM((length, 128), jnp.float32),
                pltpu.VMEM((length, 128), jnp.float32),
            ],
        ),
        out_shape=jax.ShapeDtypeStruct((length, width), jnp.bfloat16),
        compiler_params=pltpu.CompilerParams(vmem_limit_bytes=48 << 20),
        name="attend_back",
    )(side, slopes, joint, joint, joint, far, logs, mixed, grads)


def one_device(
    tokens,
    blocks,
    first_gain,
    first_shift,
    joint_weight,
    joint_bias,
    output_weight,
    output_bias,
    second_gain,
    second_shift,
    upward_weight,
    upward_bias,
    downward_weight,
    downward_bias,
    cotangent,
):
    groups = lax.axis_size("seq")
    shards = lax.axis_size("fsdp")
    side = lax.axis_index("seq")
    half_tokens = tokens.shape[1]
    width = tokens.shape[2]
    rows = joint_weight.shape[0]
    length = half_tokens * groups
    local_heads = HEADS // groups
    part = width // groups
    hidden_rows = downward_weight.shape[0]
    unit = hidden_rows // groups
    wide = 3 * part
    f32 = jnp.float32
    bf16 = jnp.bfloat16

    def swap(x):
        return lax.ppermute(x, "seq", [(s, groups - 1 - s) for s in range(groups)])

    def pick(x, axis, which=side):
        return lax.dynamic_index_in_dim(x, which, axis, keepdims=False)

    def gather(x):
        return lax.all_gather(x, "fsdp", axis=0, tiled=True)

    def scatter(x):
        return lax.psum_scatter(x, "fsdp", scatter_dimension=0, tiled=True)

    def weave(own, other, axis):
        return jnp.where(
            side == 0, jnp.stack([own, other], axis), jnp.stack([other, own], axis)
        )

    def tie(*xs):
        return lax.optimization_barrier(xs)

    place = lax.axis_index("fsdp")
    bits = [1 << n for n in reversed(range((shards - 1).bit_length()))]

    def exchange(x, bit):
        return lax.ppermute(x, "fsdp", [(s, s ^ bit) for s in range(shards)])

    def merge(x, other, level):
        return jnp.where(
            place & bits[level] == 0,
            jnp.stack([x, other], level),
            jnp.stack([other, x], level),
        )

    def tree_gather(x, levels):
        for level in levels:
            x = merge(x, exchange(x, bits[level]), level)
        return x

    def tree_step(x, level):
        mine = (place // bits[level]) % 2
        other = exchange(pick(x, level, 1 - mine), bits[level])
        return (pick(x, level, mine).astype(f32) + other.astype(f32)).astype(x.dtype)

    def tree_shape(x):
        return x.reshape((2,) * len(bits) + x.shape[1:])

    token_own = tokens[0]
    grad_own = cotangent[0]
    token_other = swap(token_own)
    grad_other = swap(grad_own)

    vectors = jnp.concatenate(
        [
            first_gain,
            first_shift,
            joint_bias[0],
            joint_bias[1],
            output_bias,
            second_gain,
            second_shift,
            downward_bias,
            upward_bias,
        ]
    )
    depth = len(bits)
    vector_full = tree_gather(vectors[None], range(depth)).reshape(shards, -1).astype(f32)
    joint_part = pick(joint_weight.reshape(rows, 3, groups, part), 2).reshape(rows, wide)
    joint_full = gather(joint_part)
    up_part = pick(upward_weight.reshape(rows, shards, groups, unit), 2)
    up_part = up_part.reshape(rows, shards * unit)
    up_full = gather(up_part)
    out_tree = tree_gather(output_weight, range(depth - 1))
    down_part = pick(downward_weight.reshape(groups, unit, width), 0)
    out_tree, down_part = tie(out_tree, down_part)
    out_full = tree_gather(out_tree, range(depth - 1, depth)).reshape(width, width)
    down_tree = tree_gather(down_part, range(depth - 3))

    def vector(index):
        return vector_full[:, index * rows : (index + 1) * rows].reshape(width)

    gain_one, shift_one, query_bias, value_bias = (vector(n) for n in range(4))
    out_bias, gain_two, shift_two, down_bias = (vector(n) for n in range(4, 8))
    up_bias = vector_full[:, 8 * rows : 8 * rows + hidden_rows].reshape(shards, groups, unit)
    up_bias = pick(up_bias, 1).reshape(shards * unit)
    joint_bias_part = jnp.concatenate(
        [
            pick(query_bias.reshape(groups, part), 0),
            jnp.zeros((part,), f32),
            pick(value_bias.reshape(groups, part), 0),
        ]
    )

    inputs = jnp.concatenate([token_own, token_other], axis=0).astype(f32)
    xhat_one, rate_one = standardize(inputs)
    normed_one = (xhat_one * gain_one + shift_one).astype(bf16)
    joint = (matmul(normed_one, joint_full) + joint_bias_part).astype(bf16)

    positions = jnp.arange(length)
    distance = jnp.abs(positions[:, None] - positions[None, :]).astype(f32)
    block_row = blocks[0]
    far = jnp.where(block_row[:, None] <= block_row[None, :], distance, FAR)
    head_index = side * local_heads + jnp.arange(local_heads)
    slopes = jnp.exp2(-8.0 * (head_index.astype(f32) + 1.0) / HEADS)
    side_array = side.astype(jnp.int32).reshape(1)
    pairs = part // 128
    calls = 2
    chunk = pairs // calls
    own_parts, other_parts, log_parts = [], [], []
    for call in range(calls):
        mixed_part, log_part = attend_heads(
            joint, side_array, slopes, far, call * chunk, chunk
        )
        other = swap(mixed_part)
        level = depth - 3 + call
        down_other = exchange(down_tree, bits[level])
        down_other, mixed_part, joint = tie(down_other, mixed_part, joint)
        down_tree = merge(down_tree, down_other, level)
        own_parts.append(mixed_part)
        log_parts.append(log_part)
        other_parts.append(jnp.concatenate([other[half_tokens:], other[:half_tokens]], axis=0))
    logs = jnp.concatenate(log_parts, axis=0)
    mixed_own = jnp.concatenate(own_parts, axis=1)
    mixed = jnp.where(
        side == 0,
        jnp.concatenate(own_parts + other_parts, axis=1),
        jnp.concatenate(other_parts + own_parts, axis=1),
    )
    hidden = inputs + matmul(mixed, out_full) + out_bias
    xhat_two, rate_two = standardize(hidden)
    normed_two = (xhat_two * gain_two + shift_two).astype(bf16)
    upward = matmul(normed_two, up_full) + up_bias
    activated = gelu_tanh(upward).astype(bf16)
    down_other = exchange(down_tree, bits[depth - 1])
    down_other, activated = tie(down_other, activated)
    down_full = merge(down_tree, down_other, depth - 1).reshape(shards * unit, width)

    grad_low = jnp.concatenate([grad_own, grad_other], axis=0)
    grad_down = left_contract(activated, grad_low).astype(bf16)
    down_full, grad_down = lax.optimization_barrier((down_full, grad_down))
    grad_down = scatter(grad_down)

    def feed_back(grad, before):
        grad_act = right_contract(grad, down_full)
        grad_up = jax.vjp(gelu_tanh, before)[1](grad_act)[0].astype(bf16)
        return grad_up, right_contract(grad_up, up_full)

    grad_up_far, grad_two_far = feed_back(grad_other, upward[half_tokens:])
    grad_two_low, grad_near = lax.optimization_barrier((grad_two_far.astype(bf16), grad_own))
    grad_two_other = swap(grad_two_low)
    grad_up_near, grad_two_near = feed_back(grad_near, upward[:half_tokens])
    grad_up = jnp.concatenate([grad_up_near, grad_up_far], axis=0)
    grad_up_weight = left_contract(normed_two, grad_up).astype(bf16)
    gain_two_sum = jnp.sum(grad_two_near * xhat_two[:half_tokens], axis=0) + jnp.sum(
        grad_two_far * xhat_two[half_tokens:], axis=0
    )
    shift_two_sum = jnp.sum(grad_two_near, axis=0) + jnp.sum(grad_two_far, axis=0)
    grad_two_other, grad_up_weight, gain_two_sum, shift_two_sum = tie(
        grad_two_other, grad_up_weight, gain_two_sum, shift_two_sum
    )
    grad_up_weight = scatter(grad_up_weight)
    grad_two_own = grad_two_near + grad_two_other.astype(f32)
    grad_hidden = grad_own.astype(f32) + norm_back(
        grad_two_own, gain_two, xhat_two[:half_tokens], rate_two[:half_tokens]
    )
    hidden_low = grad_hidden.astype(bf16)

    grad_mixed = right_contract(hidden_low, out_full).astype(bf16)
    mixed_parts = grad_mixed.reshape(half_tokens, groups, part)
    grad_heads_other = swap(pick(mixed_parts, 1, groups - 1 - side))
    late_activated, mixed_parts = lax.optimization_barrier((activated, mixed_parts))
    partial_out = matmul(late_activated, down_full)
    partial_own = partial_out[:half_tokens]
    partial_other = partial_out[half_tokens:].astype(bf16)
    grad_heads_other, partial_other, hidden_late = lax.optimization_barrier(
        (grad_heads_other, partial_other, hidden_low)
    )
    low_parts = hidden_late.reshape(half_tokens, groups, part)
    low_other = swap(pick(low_parts, 1, groups - 1 - side))
    result_other = swap(partial_other)
    grad_heads = jnp.concatenate([pick(mixed_parts, 1), grad_heads_other], axis=0)
    grad_joint = attend_back(joint, side_array, slopes, far, logs, mixed_own, grad_heads)
    grad_joint, low_other = lax.optimization_barrier((grad_joint, low_other))

    low_columns = jnp.concatenate([pick(low_parts, 1), low_other], axis=0)
    grad_out = left_contract(mixed, low_columns).astype(bf16)
    result = hidden[:half_tokens] + partial_own + result_other.astype(f32) + down_bias

    grad_joint_weight = left_contract(normed_one, grad_joint).astype(bf16)
    last = jnp.concatenate([grad_joint_weight, grad_out], axis=1)
    last = last.reshape(shards, rows, wide + part)
    grad_joint, last, grad_down = lax.optimization_barrier((grad_joint, last, grad_down))
    last = tree_step(tree_shape(last), depth - 1)
    grad_one_far = right_contract(grad_joint[half_tokens:], joint_full)
    grad_one_other = swap(grad_one_far.astype(bf16))
    grad_one_near = right_contract(grad_joint[:half_tokens], joint_full)
    last = tree_step(last, depth - 2)

    def spread(x):
        empty = jnp.zeros_like(x)
        return weave(x, empty, 0).reshape(width)

    joint_sums = jnp.sum(grad_joint.astype(f32), axis=0)
    sums = [
        jnp.sum(grad_one_near * xhat_one[:half_tokens], axis=0)
        + jnp.sum(grad_one_far * xhat_one[half_tokens:], axis=0),
        jnp.sum(grad_one_near, axis=0) + jnp.sum(grad_one_far, axis=0),
        spread(joint_sums[:part]),
        spread(joint_sums[2 * part :]),
        jnp.sum(hidden_low.astype(f32), axis=0),
        gain_two_sum,
        shift_two_sum,
        jnp.sum(grad_own.astype(f32), axis=0),
    ]
    up_sums = jnp.sum(grad_up.astype(f32), axis=0).reshape(shards, unit)
    up_sums = weave(up_sums, jnp.zeros_like(up_sums), 1).reshape(shards, hidden_rows)
    sum_rows = jnp.concatenate([s.reshape(shards, rows) for s in sums] + [up_sums], axis=1)
    sum_tree = tree_step(tree_shape(sum_rows[:, None]), depth - 1)
    last, sum_tree, grad_one_other, grad_up_weight = tie(
        last, sum_tree, grad_one_other, grad_up_weight
    )
    for level in reversed(range(depth - 2)):
        last = tree_step(last, level)
        sum_tree = tree_step(sum_tree, level + 1)
        last, sum_tree = tie(last, sum_tree)
    last_other = swap(last)
    vector_total = tree_step(sum_tree, 0)[0]
    vector_total = vector_total + swap(vector_total)

    grad_one_own = grad_one_near + grad_one_other.astype(f32)
    grad_tokens = grad_hidden + norm_back(
        grad_one_own, gain_one, xhat_one[:half_tokens], rate_one[:half_tokens]
    )

    down_total = weave(grad_down, swap(grad_down), 0).reshape(hidden_rows, width)
    up_own = grad_up_weight.reshape(rows, shards, unit)
    up_other = swap(grad_up_weight).reshape(rows, shards, unit)
    up_total = weave(up_own, up_other, 2).reshape(rows, shards * hidden_rows)
    joint_total = weave(
        last[:, :wide].reshape(rows, 3, part), last_other[:, :wide].reshape(rows, 3, part), 2
    ).reshape(rows, 3 * width)
    out_total = weave(last[:, wide:], last_other[:, wide:], 1).reshape(rows, width)

    def total(index):
        return vector_total[index * rows : (index + 1) * rows]

    return (
        result.astype(bf16)[None],
        grad_tokens[None],
        total(0),
        total(1),
        joint_total.astype(f32),
        jnp.stack([total(2), total(3)]),
        out_total.astype(f32),
        total(4),
        total(5),
        total(6),
        up_total.astype(f32),
        vector_total[8 * rows : 8 * rows + hidden_rows],
        down_total.astype(f32),
        total(7),
    )


def solution(mesh):
    in_specs = (
        P("fsdp", "seq", None),
        P("fsdp", None),
        P("fsdp"),
        P("fsdp"),
        P("fsdp", None),
        P(None, "fsdp"),
        P("fsdp", None),
        P("fsdp"),
        P("fsdp"),
        P("fsdp"),
        P("fsdp", None),
        P("fsdp"),
        P("fsdp", None),
        P("fsdp"),
        P("fsdp", "seq", None),
    )
    out_specs = (
        P("fsdp", "seq", None),
        P("fsdp", "seq", None),
        P("fsdp"),
        P("fsdp"),
        P("fsdp", None),
        P(None, "fsdp"),
        P("fsdp", None),
        P("fsdp"),
        P("fsdp"),
        P("fsdp"),
        P("fsdp", None),
        P("fsdp"),
        P("fsdp", None),
        P("fsdp"),
    )
    return jax.shard_map(
        one_device, mesh=mesh, in_specs=in_specs, out_specs=out_specs, check_vma=False
    )
```

```python
import functools

import jax
import jax.numpy as jnp
from jax import lax
from jax.experimental import pallas as pl
from jax.experimental.pallas import tpu as pltpu
from jax.sharding import PartitionSpec as P


HEADS = 16
HEAD_DIM = 64
TILE = 256
EPSILON = 1e-05
FAR = 1e30


def gelu_tanh(values):
    return jax.nn.gelu(values, approximate=True)


def matmul(left, right):
    return jnp.dot(left, right, preferred_element_type=jnp.float32)


def left_contract(left, right):
    return lax.dot_general(
        left, right, (((0,), (0,)), ((), ())), preferred_element_type=jnp.float32
    )


def right_contract(left, right):
    return lax.dot_general(
        left, right, (((1,), (1,)), ((), ())), preferred_element_type=jnp.float32
    )


def standardize(values):
    center = values - jnp.mean(values, axis=-1, keepdims=True)
    spread = jnp.mean(center * center, axis=-1, keepdims=True)
    rate = lax.rsqrt(spread + EPSILON)
    return center * rate, rate


def norm_back(grad, gain, xhat, rate):
    e = grad * gain
    mean_e = jnp.mean(e, axis=-1, keepdims=True)
    mean_ex = jnp.mean(e * xhat, axis=-1, keepdims=True)
    return (e - mean_e - xhat * mean_ex) * rate


def half_starts(side, half):
    first = pl.multiple_of(side * half, half)
    second = pl.multiple_of(half - side * half, half)
    return first, second


def in_order(ref, first, second, half):
    return jnp.concatenate([ref[pl.ds(first, half), :], ref[pl.ds(second, half), :]], axis=0)


def tile_start(g, first, second, half):
    per_half = half // TILE
    base = first if g < per_half else second
    return pl.multiple_of(base + (g % per_half) * TILE, TILE)


def pad_head(x, a):
    zeros = jnp.zeros((HEAD_DIM, x.shape[1]), x.dtype)
    mine = x[a * HEAD_DIM : (a + 1) * HEAD_DIM]
    return jnp.concatenate([mine, zeros] if a == 0 else [zeros, mine], axis=0)


def attend_kernel(begin, side_ref, slope_ref, q_ref, k_ref, v_ref, far_ref, out_ref, log_ref):
    length = q_ref.shape[0]
    half = length // 2
    pair = pl.program_id(0) + begin
    first, second = half_starts(side_ref[0], half)
    keys = in_order(k_ref, first, second, half)
    values_t = in_order(v_ref, first, second, half).T
    for g in range(length // TILE):
        reach = min((g + 2) * TILE, length)
        start = tile_start(g, first, second, half)
        queries_t = (q_ref[pl.ds(start, TILE), :] * jnp.bfloat16(HEAD_DIM ** (-0.5))).T
        pieces = []
        for a in range(2):
            slope = slope_ref[2 * pair + a]
            scores = matmul(keys[:reach], pad_head(queries_t, a))
            scores = scores - slope * far_ref[:reach, g * TILE : (g + 1) * TILE]
            top = jnp.max(scores, axis=0, keepdims=True)
            weights = jnp.exp(scores - top)
            total = jnp.sum(weights, axis=0, keepdims=True)
            mixed_t = matmul(
                values_t[a * HEAD_DIM : (a + 1) * HEAD_DIM, :reach], weights.astype(jnp.bfloat16)
            )
            pieces.append(mixed_t / total)
            log_ref[0, a : a + 1, g * TILE : (g + 1) * TILE] = top + jnp.log(total)
        out_ref[pl.ds(start, TILE), :] = jnp.concatenate(pieces, axis=0).T.astype(jnp.bfloat16)


def attend_heads(joint, side, slopes, far, begin, count):
    length, width = joint.shape
    pairs = width // 3 // 128
    whole = lambda offset: pl.BlockSpec((length, 128), lambda p, s: (0, p + offset))
    return pl.pallas_call(
        functools.partial(attend_kernel, begin),
        grid_spec=pltpu.PrefetchScalarGridSpec(
            num_scalar_prefetch=1,
            grid=(count,),
            in_specs=[
                pl.BlockSpec(memory_space=pltpu.SMEM),
                whole(begin),
                whole(begin + pairs),
                whole(begin + 2 * pairs),
                pl.BlockSpec((length, length), lambda p, s: (0, 0)),
            ],
            out_specs=[
                pl.BlockSpec((length, 128), lambda p, s: (0, p)),
                pl.BlockSpec((1, 2, length), lambda p, s: (p, 0, 0)),
            ],
        ),
        out_shape=[
            jax.ShapeDtypeStruct((length, count * 128), jnp.bfloat16),
            jax.ShapeDtypeStruct((count, 2, length), jnp.float32),
        ],
        compiler_params=pltpu.CompilerParams(vmem_limit_bytes=48 << 20),
        name="attend",
    )(side, slopes, joint, joint, joint, far)


def back_kernel(
    side_ref,
    slope_ref,
    q_ref,
    k_ref,
    v_ref,
    far_ref,
    log_ref,
    mixed_ref,
    grad_ref,
    out_ref,
    dq_ref,
    dk_ref,
    dv_ref,
):
    length = q_ref.shape[0]
    half = length // 2
    pair = pl.program_id(0)
    part = pl.program_id(1)
    first, second = half_starts(side_ref[0], half)
    factor = HEAD_DIM ** (-0.5)

    @pl.when(part == 0)
    def _():
        keys = in_order(k_ref, first, second, half)
        keys_t = keys.T
        values = in_order(v_ref, first, second, half)
        lane = lax.broadcasted_iota(jnp.int32, (TILE, 128), 1)
        dk_ref[...] = jnp.zeros_like(dk_ref)
        dv_ref[...] = jnp.zeros_like(dv_ref)
        for g in range(length // TILE):
            reach = min((g + 2) * TILE, length)
            start = tile_start(g, first, second, half)
            queries = q_ref[pl.ds(start, TILE), :] * jnp.bfloat16(factor)
            queries_t = queries.T
            grads = grad_ref[pl.ds(start, TILE), :]
            grads_t = grads.T
            product = grads.astype(jnp.float32) * mixed_ref[pl.ds(start, TILE), :].astype(
                jnp.float32
            )
            product_t = product.T
            pieces = []
            for a in range(2):
                rows = slice(a * HEAD_DIM, (a + 1) * HEAD_DIM)
                slope = slope_ref[2 * pair + a]
                own = (lane < HEAD_DIM) if a == 0 else (lane >= HEAD_DIM)
                scores = matmul(keys[:reach], pad_head(queries_t, a))
                scores = scores - slope * far_ref[:reach, g * TILE : (g + 1) * TILE]
                probs = jnp.exp(scores - log_ref[0, a : a + 1, g * TILE : (g + 1) * TILE])
                grad_probs = matmul(values[:reach], pad_head(grads_t, a))
                inner = jnp.sum(product_t[rows], axis=0, keepdims=True)
                grad_scores = (probs * (grad_probs - inner)).astype(jnp.bfloat16)
                zero = jnp.zeros((), jnp.bfloat16)
                dk_ref[:reach] += matmul(grad_scores, jnp.where(own, queries, zero))
                dv_ref[:reach] += matmul(probs.astype(jnp.bfloat16), jnp.where(own, grads, zero))
                pieces.append(matmul(keys_t[rows, :reach], grad_scores))
            both = jnp.concatenate(pieces, axis=0).T * factor
            dq_ref[pl.ds(start, TILE), :] = both.astype(jnp.bfloat16)
        out_ref[...] = dq_ref[...]

    @pl.when(part == 1)
    def _():
        out_ref[pl.ds(first, half), :] = dk_ref[:half].astype(jnp.bfloat16)
        out_ref[pl.ds(second, half), :] = dk_ref[half:].astype(jnp.bfloat16)

    @pl.when(part == 2)
    def _():
        out_ref[pl.ds(first, half), :] = dv_ref[:half].astype(jnp.bfloat16)
        out_ref[pl.ds(second, half), :] = dv_ref[half:].astype(jnp.bfloat16)


def attend_back(joint, side, slopes, far, logs, mixed, grads):
    length, width = joint.shape
    pairs = width // 3 // 128
    whole = lambda offset: pl.BlockSpec((length, 128), lambda p, t, s: (0, p + offset))
    return pl.pallas_call(
        back_kernel,
        grid_spec=pltpu.PrefetchScalarGridSpec(
            num_scalar_prefetch=1,
            grid=(pairs, 3),
            in_specs=[
                pl.BlockSpec(memory_space=pltpu.SMEM),
                whole(0),
                whole(pairs),
                whole(2 * pairs),
                pl.BlockSpec((length, length), lambda p, t, s: (0, 0)),
                pl.BlockSpec((1, 2, length), lambda p, t, s: (p, 0, 0)),
                whole(0),
                whole(0),
            ],
            out_specs=pl.BlockSpec((length, 128), lambda p, t, s: (0, t * pairs + p)),
            scratch_shapes=[
                pltpu.VMEM((length, 128), jnp.bfloat16),
                pltpu.VMEM((length, 128), jnp.float32),
                pltpu.VMEM((length, 128), jnp.float32),
            ],
        ),
        out_shape=jax.ShapeDtypeStruct((length, width), jnp.bfloat16),
        compiler_params=pltpu.CompilerParams(vmem_limit_bytes=48 << 20),
        name="attend_back",
    )(side, slopes, joint, joint, joint, far, logs, mixed, grads)


def one_device(
    tokens,
    blocks,
    first_gain,
    first_shift,
    joint_weight,
    joint_bias,
    output_weight,
    output_bias,
    second_gain,
    second_shift,
    upward_weight,
    upward_bias,
    downward_weight,
    downward_bias,
    cotangent,
):
    groups = lax.axis_size("seq")
    shards = lax.axis_size("fsdp")
    side = lax.axis_index("seq")
    half_tokens = tokens.shape[1]
    width = tokens.shape[2]
    rows = joint_weight.shape[0]
    length = half_tokens * groups
    local_heads = HEADS // groups
    part = width // groups
    hidden_rows = downward_weight.shape[0]
    unit = hidden_rows // groups
    wide = 3 * part
    f32 = jnp.float32
    bf16 = jnp.bfloat16

    def swap(x):
        return lax.ppermute(x, "seq", [(s, groups - 1 - s) for s in range(groups)])

    def pick(x, axis, which=side):
        return lax.dynamic_index_in_dim(x, which, axis, keepdims=False)

    def gather(x):
        return lax.all_gather(x, "fsdp", axis=0, tiled=True)

    def scatter(x):
        return lax.psum_scatter(x, "fsdp", scatter_dimension=0, tiled=True)

    def weave(own, other, axis):
        return jnp.where(
            side == 0, jnp.stack([own, other], axis), jnp.stack([other, own], axis)
        )

    def tie(*xs):
        return lax.optimization_barrier(xs)

    place = lax.axis_index("fsdp")
    bits = [1 << n for n in reversed(range((shards - 1).bit_length()))]

    def exchange(x, bit):
        return lax.ppermute(x, "fsdp", [(s, s ^ bit) for s in range(shards)])

    def merge(x, other, level):
        return jnp.where(
            place & bits[level] == 0,
            jnp.stack([x, other], level),
            jnp.stack([other, x], level),
        )

    def tree_gather(x, levels):
        for level in levels:
            x = merge(x, exchange(x, bits[level]), level)
        return x

    def tree_step(x, level):
        mine = (place // bits[level]) % 2
        other = exchange(pick(x, level, 1 - mine), bits[level])
        return (pick(x, level, mine).astype(f32) + other.astype(f32)).astype(x.dtype)

    def tree_shape(x):
        return x.reshape((2,) * len(bits) + x.shape[1:])

    token_own = tokens[0]
    grad_own = cotangent[0]
    token_other = swap(token_own)
    grad_other = swap(grad_own)

    vectors = jnp.concatenate(
        [
            first_gain,
            first_shift,
            joint_bias[0],
            joint_bias[1],
            output_bias,
            second_gain,
            second_shift,
            downward_bias,
            upward_bias,
        ]
    )
    depth = len(bits)
    vector_full = tree_gather(vectors[None], range(depth)).reshape(shards, -1).astype(f32)
    joint_part = jnp.concatenate(
        [
            lax.dynamic_slice_in_dim(joint_weight, n * width + side * part, part, axis=1)
            for n in range(3)
        ],
        axis=1,
    )
    joint_full = gather(joint_part)
    up_part = pick(upward_weight.reshape(rows, shards, groups, unit), 2)
    up_part = up_part.reshape(rows, shards * unit)
    up_full = gather(up_part)
    out_tree = tree_gather(output_weight, range(depth - 2))
    down_part = pick(downward_weight.reshape(groups, unit, width), 0)
    out_tree, down_part = tie(out_tree, down_part)
    out_full = tree_gather(out_tree, range(depth - 2, depth)).reshape(width, width)
    down_tree = tree_gather(down_part, range(depth - 4))
    down_first = exchange(down_tree, bits[depth - 4])

    def vector(index):
        return vector_full[:, index * rows : (index + 1) * rows].reshape(width)

    gain_one, shift_one, query_bias, value_bias = (vector(n) for n in range(4))
    out_bias, gain_two, shift_two, down_bias = (vector(n) for n in range(4, 8))
    up_bias = vector_full[:, 8 * rows : 8 * rows + hidden_rows].reshape(shards, groups, unit)
    up_bias = pick(up_bias, 1).reshape(shards * unit)
    joint_bias_part = jnp.concatenate(
        [
            pick(query_bias.reshape(groups, part), 0),
            jnp.zeros((part,), f32),
            pick(value_bias.reshape(groups, part), 0),
        ]
    )

    inputs = jnp.concatenate([token_own, token_other], axis=0).astype(f32)
    xhat_one, rate_one = standardize(inputs)
    normed_one = (xhat_one * gain_one + shift_one).astype(bf16)
    joint = (matmul(normed_one, joint_full) + joint_bias_part).astype(bf16)

    down_tree = merge(down_tree, tie(down_first, joint)[0], depth - 4)

    positions = jnp.arange(length)
    distance = jnp.abs(positions[:, None] - positions[None, :]).astype(f32)
    block_row = blocks[0]
    far = jnp.where(block_row[:, None] <= block_row[None, :], distance, FAR)
    head_index = side * local_heads + jnp.arange(local_heads)
    slopes = jnp.exp2(-8.0 * (head_index.astype(f32) + 1.0) / HEADS)
    side_array = side.astype(jnp.int32).reshape(1)
    pairs = part // 128
    calls = 2
    chunk = pairs // calls
    own_parts, other_parts, log_parts = [], [], []
    for call in range(calls):
        mixed_part, log_part = attend_heads(
            joint, side_array, slopes, far, call * chunk, chunk
        )
        other = swap(mixed_part)
        level = depth - 3 + call
        down_other = exchange(down_tree, bits[level])
        down_tree = merge(down_tree, tie(down_other, mixed_part)[0], level)
        own_parts.append(mixed_part)
        log_parts.append(log_part)
        other_parts.append(jnp.concatenate([other[half_tokens:], other[:half_tokens]], axis=0))
    logs = jnp.concatenate(log_parts, axis=0)
    mixed_own = jnp.concatenate(own_parts, axis=1)
    mixed = jnp.where(
        side == 0,
        jnp.concatenate(own_parts + other_parts, axis=1),
        jnp.concatenate(other_parts + own_parts, axis=1),
    )
    hidden = inputs + matmul(mixed, out_full) + out_bias
    xhat_two, rate_two = standardize(hidden)
    normed_two = (xhat_two * gain_two + shift_two).astype(bf16)
    upward = matmul(normed_two, up_full) + up_bias
    activated = gelu_tanh(upward).astype(bf16)
    down_other = exchange(down_tree, bits[depth - 1])
    down_full = merge(down_tree, tie(down_other, activated)[0], depth - 1).reshape(shards * unit, width)

    grad_low = jnp.concatenate([grad_own, grad_other], axis=0)
    grad_down = left_contract(activated, grad_low).astype(bf16)
    down_full, grad_down = lax.optimization_barrier((down_full, grad_down))
    grad_down = scatter(grad_down)

    def feed_back(grad, before):
        grad_act = right_contract(grad, down_full)
        grad_up = jax.vjp(gelu_tanh, before)[1](grad_act)[0].astype(bf16)
        return grad_up, right_contract(grad_up, up_full)

    grad_up_far, grad_two_far = feed_back(grad_other, upward[half_tokens:])
    grad_two_low, grad_near = lax.optimization_barrier((grad_two_far.astype(bf16), grad_own))
    grad_two_other = swap(grad_two_low)
    grad_up_near, grad_two_near = feed_back(grad_near, upward[:half_tokens])
    grad_up = jnp.concatenate([grad_up_near, grad_up_far], axis=0)
    grad_up_weight = left_contract(normed_two, grad_up).astype(bf16)
    gain_two_sum = jnp.sum(grad_two_near * xhat_two[:half_tokens], axis=0) + jnp.sum(
        grad_two_far * xhat_two[half_tokens:], axis=0
    )
    shift_two_sum = jnp.sum(grad_two_near, axis=0) + jnp.sum(grad_two_far, axis=0)
    late_activated = tie(activated, grad_up_near)[0]
    partial_out = matmul(late_activated, down_full)
    partial_own = partial_out[:half_tokens]
    partial_other = partial_out[half_tokens:].astype(bf16)
    grad_two_other = tie(
        grad_two_other, grad_up_weight, gain_two_sum, shift_two_sum, partial_out
    )[0]
    grad_up_weight = scatter(grad_up_weight)
    grad_two_own = grad_two_near + grad_two_other.astype(f32)
    grad_hidden = grad_own.astype(f32) + norm_back(
        grad_two_own, gain_two, xhat_two[:half_tokens], rate_two[:half_tokens]
    )
    hidden_low = grad_hidden.astype(bf16)

    grad_mixed = right_contract(hidden_low, out_full).astype(bf16)
    mixed_parts = grad_mixed.reshape(half_tokens, groups, part)
    grad_heads_other = swap(pick(mixed_parts, 1, groups - 1 - side))
    low_parts = tie(hidden_low, mixed_parts)[0].reshape(half_tokens, groups, part)
    low_other = swap(pick(low_parts, 1, groups - 1 - side))
    partial_other = tie(partial_other, grad_heads_other)[0]
    result_other = swap(partial_other)
    grad_heads = jnp.concatenate([pick(mixed_parts, 1), grad_heads_other], axis=0)
    grad_joint = attend_back(joint, side_array, slopes, far, logs, mixed_own, grad_heads)
    low_other = tie(low_other, grad_joint)[0]
    low_sum = jnp.sum(tie(hidden_low, grad_joint)[0].astype(f32), axis=0)

    low_columns = jnp.concatenate([pick(low_parts, 1), low_other], axis=0)
    grad_out = left_contract(mixed, low_columns).astype(bf16)
    result = hidden[:half_tokens] + partial_own + result_other.astype(f32) + down_bias

    grad_joint_weight = left_contract(normed_one, grad_joint).astype(bf16)
    last = jnp.concatenate([grad_joint_weight, grad_out], axis=1)
    last = last.reshape(shards, rows, wide + part)
    grad_joint, last, grad_down = lax.optimization_barrier((grad_joint, last, grad_down))
    last = tree_step(tree_shape(last), depth - 1)
    grad_one_far = right_contract(grad_joint[half_tokens:], joint_full)
    grad_one_other = swap(grad_one_far.astype(bf16))
    grad_one_near = right_contract(grad_joint[:half_tokens], joint_full)
    last = tree_step(last, depth - 2)

    def spread(x):
        empty = jnp.zeros_like(x)
        return weave(x, empty, 0).reshape(width)

    joint_sums = jnp.sum(grad_joint.astype(f32), axis=0)
    sums = [
        jnp.sum(grad_one_near * xhat_one[:half_tokens], axis=0)
        + jnp.sum(grad_one_far * xhat_one[half_tokens:], axis=0),
        jnp.sum(grad_one_near, axis=0) + jnp.sum(grad_one_far, axis=0),
        spread(joint_sums[:part]),
        spread(joint_sums[2 * part :]),
        low_sum,
        gain_two_sum,
        shift_two_sum,
        jnp.sum(grad_own.astype(f32), axis=0),
    ]
    up_sums = jnp.sum(grad_up.astype(f32), axis=0).reshape(shards, unit)
    up_sums = weave(up_sums, jnp.zeros_like(up_sums), 1).reshape(shards, hidden_rows)
    sum_rows = jnp.concatenate([s.reshape(shards, rows) for s in sums] + [up_sums], axis=1)
    sum_tree = tree_step(tree_shape(sum_rows[:, None]), depth - 1)
    last, sum_tree, grad_one_other, grad_up_weight = tie(
        last, sum_tree, grad_one_other, grad_up_weight
    )
    for level in reversed(range(depth - 2)):
        last = tree_step(last, level)
        sum_tree = tree_step(sum_tree, level + 1)
        last, sum_tree = tie(last, sum_tree)
    last_other = swap(last)
    vector_total = tree_step(sum_tree, 0)[0]
    vector_total = vector_total + swap(vector_total)

    grad_one_own = grad_one_near + grad_one_other.astype(f32)
    grad_tokens = grad_hidden + norm_back(
        grad_one_own, gain_one, xhat_one[:half_tokens], rate_one[:half_tokens]
    )

    down_total = weave(grad_down, swap(grad_down), 0).reshape(hidden_rows, width)
    up_own = grad_up_weight.reshape(rows, shards, unit)
    up_other = swap(grad_up_weight).reshape(rows, shards, unit)
    up_total = weave(up_own, up_other, 2).reshape(rows, shards * hidden_rows)
    joint_total = weave(
        last[:, :wide].reshape(rows, 3, part), last_other[:, :wide].reshape(rows, 3, part), 2
    ).reshape(rows, 3 * width)
    out_total = weave(last[:, wide:], last_other[:, wide:], 1).reshape(rows, width)

    def total(index):
        return vector_total[index * rows : (index + 1) * rows]

    return (
        result.astype(bf16)[None],
        grad_tokens[None],
        total(0),
        total(1),
        joint_total.astype(f32),
        jnp.stack([total(2), total(3)]),
        out_total.astype(f32),
        total(4),
        total(5),
        total(6),
        up_total.astype(f32),
        vector_total[8 * rows : 8 * rows + hidden_rows],
        down_total.astype(f32),
        total(7),
    )


def solution(mesh):
    in_specs = (
        P("fsdp", "seq", None),
        P("fsdp", None),
        P("fsdp"),
        P("fsdp"),
        P("fsdp", None),
        P(None, "fsdp"),
        P("fsdp", None),
        P("fsdp"),
        P("fsdp"),
        P("fsdp"),
        P("fsdp", None),
        P("fsdp"),
        P("fsdp", None),
        P("fsdp"),
        P("fsdp", "seq", None),
    )
    out_specs = (
        P("fsdp", "seq", None),
        P("fsdp", "seq", None),
        P("fsdp"),
        P("fsdp"),
        P("fsdp", None),
        P(None, "fsdp"),
        P("fsdp", None),
        P("fsdp"),
        P("fsdp"),
        P("fsdp"),
        P("fsdp", None),
        P("fsdp"),
        P("fsdp", None),
        P("fsdp"),
    )
    return jax.shard_map(
        one_device, mesh=mesh, in_specs=in_specs, out_specs=out_specs, check_vma=False
    )
```

```python
import functools

import jax
import jax.numpy as jnp
from jax import lax
from jax.experimental import pallas as pl
from jax.experimental.pallas import tpu as pltpu
from jax.sharding import PartitionSpec as P


HEADS = 16
HEAD_DIM = 64
TILE = 256
EPSILON = 1e-05
FAR = 1e30


def gelu_tanh(values):
    return jax.nn.gelu(values, approximate=True)


def matmul(left, right):
    return jnp.dot(left, right, preferred_element_type=jnp.float32)


def left_contract(left, right):
    return lax.dot_general(
        left, right, (((0,), (0,)), ((), ())), preferred_element_type=jnp.float32
    )


def right_contract(left, right):
    return lax.dot_general(
        left, right, (((1,), (1,)), ((), ())), preferred_element_type=jnp.float32
    )


def standardize(values):
    center = values - jnp.mean(values, axis=-1, keepdims=True)
    spread = jnp.mean(center * center, axis=-1, keepdims=True)
    rate = lax.rsqrt(spread + EPSILON)
    return center * rate, rate


def norm_back(grad, gain, xhat, rate):
    e = grad * gain
    mean_e = jnp.mean(e, axis=-1, keepdims=True)
    mean_ex = jnp.mean(e * xhat, axis=-1, keepdims=True)
    return (e - mean_e - xhat * mean_ex) * rate


def half_starts(side, half):
    first = pl.multiple_of(side * half, half)
    second = pl.multiple_of(half - side * half, half)
    return first, second


def in_order(ref, first, second, half):
    return jnp.concatenate([ref[pl.ds(first, half), :], ref[pl.ds(second, half), :]], axis=0)


def tile_start(g, first, second, half):
    per_half = half // TILE
    base = first if g < per_half else second
    return pl.multiple_of(base + (g % per_half) * TILE, TILE)


def pad_head(x, a):
    zeros = jnp.zeros((HEAD_DIM, x.shape[1]), x.dtype)
    mine = x[a * HEAD_DIM : (a + 1) * HEAD_DIM]
    return jnp.concatenate([mine, zeros] if a == 0 else [zeros, mine], axis=0)


def attend_kernel(begin, side_ref, slope_ref, q_ref, k_ref, v_ref, far_ref, out_ref, log_ref):
    length = q_ref.shape[0]
    half = length // 2
    pair = pl.program_id(0) + begin
    first, second = half_starts(side_ref[0], half)
    keys = in_order(k_ref, first, second, half)
    values_t = in_order(v_ref, first, second, half).T
    for g in range(length // TILE):
        reach = min((g + 2) * TILE, length)
        start = tile_start(g, first, second, half)
        queries_t = (q_ref[pl.ds(start, TILE), :] * jnp.bfloat16(HEAD_DIM ** (-0.5))).T
        pieces = []
        for a in range(2):
            slope = slope_ref[2 * pair + a]
            scores = matmul(keys[:reach], pad_head(queries_t, a))
            scores = scores - slope * far_ref[:reach, g * TILE : (g + 1) * TILE]
            top = jnp.max(scores, axis=0, keepdims=True)
            weights = jnp.exp(scores - top)
            total = jnp.sum(weights, axis=0, keepdims=True)
            mixed_t = matmul(
                values_t[a * HEAD_DIM : (a + 1) * HEAD_DIM, :reach], weights.astype(jnp.bfloat16)
            )
            pieces.append(mixed_t / total)
            log_ref[0, a : a + 1, g * TILE : (g + 1) * TILE] = top + jnp.log(total)
        out_ref[pl.ds(start, TILE), :] = jnp.concatenate(pieces, axis=0).T.astype(jnp.bfloat16)


def attend_heads(joint, side, slopes, far, begin, count):
    length, width = joint.shape
    pairs = width // 3 // 128
    whole = lambda offset: pl.BlockSpec((length, 128), lambda p, s: (0, p + offset))
    return pl.pallas_call(
        functools.partial(attend_kernel, begin),
        grid_spec=pltpu.PrefetchScalarGridSpec(
            num_scalar_prefetch=1,
            grid=(count,),
            in_specs=[
                pl.BlockSpec(memory_space=pltpu.SMEM),
                whole(begin),
                whole(begin + pairs),
                whole(begin + 2 * pairs),
                pl.BlockSpec((length, length), lambda p, s: (0, 0)),
            ],
            out_specs=[
                pl.BlockSpec((length, 128), lambda p, s: (0, p)),
                pl.BlockSpec((1, 2, length), lambda p, s: (p, 0, 0)),
            ],
        ),
        out_shape=[
            jax.ShapeDtypeStruct((length, count * 128), jnp.bfloat16),
            jax.ShapeDtypeStruct((count, 2, length), jnp.float32),
        ],
        compiler_params=pltpu.CompilerParams(vmem_limit_bytes=48 << 20),
        name="attend",
    )(side, slopes, joint, joint, joint, far)


def back_kernel(
    side_ref,
    slope_ref,
    q_ref,
    k_ref,
    v_ref,
    far_ref,
    log_ref,
    mixed_ref,
    grad_ref,
    out_ref,
    dq_ref,
    dk_ref,
    dv_ref,
):
    length = q_ref.shape[0]
    half = length // 2
    pair = pl.program_id(0)
    part = pl.program_id(1)
    first, second = half_starts(side_ref[0], half)
    factor = HEAD_DIM ** (-0.5)

    @pl.when(part == 0)
    def _():
        keys = in_order(k_ref, first, second, half)
        keys_t = keys.T
        values = in_order(v_ref, first, second, half)
        lane = lax.broadcasted_iota(jnp.int32, (TILE, 128), 1)
        dk_ref[...] = jnp.zeros_like(dk_ref)
        dv_ref[...] = jnp.zeros_like(dv_ref)
        for g in range(length // TILE):
            reach = min((g + 2) * TILE, length)
            start = tile_start(g, first, second, half)
            queries = q_ref[pl.ds(start, TILE), :] * jnp.bfloat16(factor)
            queries_t = queries.T
            grads = grad_ref[pl.ds(start, TILE), :]
            grads_t = grads.T
            product = grads.astype(jnp.float32) * mixed_ref[pl.ds(start, TILE), :].astype(
                jnp.float32
            )
            product_t = product.T
            pieces = []
            for a in range(2):
                rows = slice(a * HEAD_DIM, (a + 1) * HEAD_DIM)
                slope = slope_ref[2 * pair + a]
                own = (lane < HEAD_DIM) if a == 0 else (lane >= HEAD_DIM)
                scores = matmul(keys[:reach], pad_head(queries_t, a))
                scores = scores - slope * far_ref[:reach, g * TILE : (g + 1) * TILE]
                probs = jnp.exp(scores - log_ref[0, a : a + 1, g * TILE : (g + 1) * TILE])
                grad_probs = matmul(values[:reach], pad_head(grads_t, a))
                inner = jnp.sum(product_t[rows], axis=0, keepdims=True)
                grad_scores = (probs * (grad_probs - inner)).astype(jnp.bfloat16)
                zero = jnp.zeros((), jnp.bfloat16)
                dk_ref[:reach] += matmul(grad_scores, jnp.where(own, queries, zero))
                dv_ref[:reach] += matmul(probs.astype(jnp.bfloat16), jnp.where(own, grads, zero))
                pieces.append(matmul(keys_t[rows, :reach], grad_scores))
            both = jnp.concatenate(pieces, axis=0).T * factor
            dq_ref[pl.ds(start, TILE), :] = both.astype(jnp.bfloat16)
        out_ref[...] = dq_ref[...]

    @pl.when(part == 1)
    def _():
        out_ref[pl.ds(first, half), :] = dk_ref[:half].astype(jnp.bfloat16)
        out_ref[pl.ds(second, half), :] = dk_ref[half:].astype(jnp.bfloat16)

    @pl.when(part == 2)
    def _():
        out_ref[pl.ds(first, half), :] = dv_ref[:half].astype(jnp.bfloat16)
        out_ref[pl.ds(second, half), :] = dv_ref[half:].astype(jnp.bfloat16)


def attend_back(joint, side, slopes, far, logs, mixed, grads):
    length, width = joint.shape
    pairs = width // 3 // 128
    whole = lambda offset: pl.BlockSpec((length, 128), lambda p, t, s: (0, p + offset))
    return pl.pallas_call(
        back_kernel,
        grid_spec=pltpu.PrefetchScalarGridSpec(
            num_scalar_prefetch=1,
            grid=(pairs, 3),
            in_specs=[
                pl.BlockSpec(memory_space=pltpu.SMEM),
                whole(0),
                whole(pairs),
                whole(2 * pairs),
                pl.BlockSpec((length, length), lambda p, t, s: (0, 0)),
                pl.BlockSpec((1, 2, length), lambda p, t, s: (p, 0, 0)),
                whole(0),
                whole(0),
            ],
            out_specs=pl.BlockSpec((length, 128), lambda p, t, s: (0, t * pairs + p)),
            scratch_shapes=[
                pltpu.VMEM((length, 128), jnp.bfloat16),
                pltpu.VMEM((length, 128), jnp.float32),
                pltpu.VMEM((length, 128), jnp.float32),
            ],
        ),
        out_shape=jax.ShapeDtypeStruct((length, width), jnp.bfloat16),
        compiler_params=pltpu.CompilerParams(vmem_limit_bytes=48 << 20),
        name="attend_back",
    )(side, slopes, joint, joint, joint, far, logs, mixed, grads)


def one_device(
    tokens,
    blocks,
    first_gain,
    first_shift,
    joint_weight,
    joint_bias,
    output_weight,
    output_bias,
    second_gain,
    second_shift,
    upward_weight,
    upward_bias,
    downward_weight,
    downward_bias,
    cotangent,
):
    groups = lax.axis_size("seq")
    shards = lax.axis_size("fsdp")
    side = lax.axis_index("seq")
    half_tokens = tokens.shape[1]
    width = tokens.shape[2]
    rows = joint_weight.shape[0]
    length = half_tokens * groups
    local_heads = HEADS // groups
    part = width // groups
    hidden_rows = downward_weight.shape[0]
    unit = hidden_rows // groups
    wide = 3 * part
    f32 = jnp.float32
    bf16 = jnp.bfloat16

    def swap(x):
        return lax.ppermute(x, "seq", [(s, groups - 1 - s) for s in range(groups)])

    def pick(x, axis, which=side):
        return lax.dynamic_index_in_dim(x, which, axis, keepdims=False)

    def gather(x):
        return lax.all_gather(x, "fsdp", axis=0, tiled=True)

    def scatter(x):
        return lax.psum_scatter(x, "fsdp", scatter_dimension=0, tiled=True)

    def weave(own, other, axis):
        return jnp.where(
            side == 0, jnp.stack([own, other], axis), jnp.stack([other, own], axis)
        )

    def tie(*xs):
        return lax.optimization_barrier(xs)

    place = lax.axis_index("fsdp")
    bits = [1 << n for n in reversed(range((shards - 1).bit_length()))]

    def exchange(x, bit):
        return lax.ppermute(x, "fsdp", [(s, s ^ bit) for s in range(shards)])

    def merge(x, other, level):
        return jnp.where(
            place & bits[level] == 0,
            jnp.stack([x, other], level),
            jnp.stack([other, x], level),
        )

    def tree_gather(x, levels):
        for level in levels:
            x = merge(x, exchange(x, bits[level]), level)
        return x

    def tree_step(x, level, axis=None):
        axis = level if axis is None else axis
        mine = (place // bits[level]) % 2
        other = exchange(pick(x, axis, 1 - mine), bits[level])
        return (pick(x, axis, mine).astype(f32) + other.astype(f32)).astype(x.dtype)

    def tree_shape(x):
        return x.reshape((2,) * len(bits) + x.shape[1:])

    token_own = tokens[0]
    grad_own = cotangent[0]
    token_other = swap(token_own)
    grad_other = swap(grad_own)

    vectors = jnp.concatenate(
        [
            first_gain,
            first_shift,
            joint_bias[0],
            joint_bias[1],
            output_bias,
            second_gain,
            second_shift,
            downward_bias,
            upward_bias,
        ]
    )
    depth = len(bits)
    vector_full = tree_gather(vectors[None], range(depth)).reshape(shards, -1).astype(f32)
    joint_part = jnp.concatenate(
        [
            lax.dynamic_slice_in_dim(joint_weight, n * width + side * part, part, axis=1)
            for n in range(3)
        ],
        axis=1,
    )
    joint_full = gather(joint_part)
    up_part = pick(upward_weight.reshape(rows, shards, groups, unit), 2)
    up_part = up_part.reshape(rows, shards * unit)
    up_full = gather(up_part)
    out_tree = tree_gather(output_weight, range(depth - 2))
    down_part = pick(downward_weight.reshape(groups, unit, width), 0)
    out_tree, down_part = tie(out_tree, down_part)
    out_full = tree_gather(out_tree, range(depth - 2, depth)).reshape(width, width)
    down_tree = tree_gather(down_part, range(depth - 4))
    down_first = exchange(down_tree, bits[depth - 4])

    def vector(index):
        return vector_full[:, index * rows : (index + 1) * rows].reshape(width)

    gain_one, shift_one, query_bias, value_bias = (vector(n) for n in range(4))
    out_bias, gain_two, shift_two, down_bias = (vector(n) for n in range(4, 8))
    up_bias = vector_full[:, 8 * rows : 8 * rows + hidden_rows].reshape(shards, groups, unit)
    up_bias = pick(up_bias, 1).reshape(shards * unit)
    joint_bias_part = jnp.concatenate(
        [
            pick(query_bias.reshape(groups, part), 0),
            jnp.zeros((part,), f32),
            pick(value_bias.reshape(groups, part), 0),
        ]
    )

    inputs = jnp.concatenate([token_own, token_other], axis=0).astype(f32)
    xhat_one, rate_one = standardize(inputs)
    normed_one = (xhat_one * gain_one + shift_one).astype(bf16)
    joint = (matmul(normed_one, joint_full) + joint_bias_part).astype(bf16)

    down_tree = merge(down_tree, tie(down_first, joint)[0], depth - 4)

    positions = jnp.arange(length)
    distance = jnp.abs(positions[:, None] - positions[None, :]).astype(f32)
    block_row = blocks[0]
    far = jnp.where(block_row[:, None] <= block_row[None, :], distance, FAR)
    head_index = side * local_heads + jnp.arange(local_heads)
    slopes = jnp.exp2(-8.0 * (head_index.astype(f32) + 1.0) / HEADS)
    side_array = side.astype(jnp.int32).reshape(1)
    pairs = part // 128
    calls = 2
    chunk = pairs // calls
    own_parts, other_parts, log_parts = [], [], []
    for call in range(calls):
        mixed_part, log_part = attend_heads(
            joint, side_array, slopes, far, call * chunk, chunk
        )
        other = swap(mixed_part)
        level = depth - 3 + call
        down_other = exchange(down_tree, bits[level])
        down_tree = merge(down_tree, tie(down_other, mixed_part)[0], level)
        own_parts.append(mixed_part)
        log_parts.append(log_part)
        other_parts.append(jnp.concatenate([other[half_tokens:], other[:half_tokens]], axis=0))
    logs = jnp.concatenate(log_parts, axis=0)
    mixed_own = jnp.concatenate(own_parts, axis=1)
    mixed = jnp.where(
        side == 0,
        jnp.concatenate(own_parts + other_parts, axis=1),
        jnp.concatenate(other_parts + own_parts, axis=1),
    )
    hidden = inputs + matmul(mixed, out_full) + out_bias
    xhat_two, rate_two = standardize(hidden)
    normed_two = (xhat_two * gain_two + shift_two).astype(bf16)
    upward = matmul(normed_two, up_full) + up_bias
    activated = gelu_tanh(upward).astype(bf16)
    down_other = exchange(down_tree, bits[depth - 1])
    down_full = merge(down_tree, tie(down_other, activated)[0], depth - 1).reshape(shards * unit, width)

    grad_low = jnp.concatenate([grad_own, grad_other], axis=0)
    grad_down = left_contract(activated, grad_low).astype(bf16)
    down_full = tie(down_full, grad_down)[0]
    grad_down = scatter(grad_down)

    def feed_back(grad, before):
        grad_act = right_contract(grad, down_full)
        grad_up = jax.vjp(gelu_tanh, before)[1](grad_act)[0].astype(bf16)
        return grad_up, right_contract(grad_up, up_full)

    grad_up_far, grad_two_far = feed_back(grad_other, upward[half_tokens:])
    grad_two_low, grad_near = lax.optimization_barrier((grad_two_far.astype(bf16), grad_own))
    grad_two_other = swap(grad_two_low)
    grad_up_near, grad_two_near = feed_back(grad_near, upward[:half_tokens])
    grad_up = jnp.concatenate([grad_up_near, grad_up_far], axis=0)
    grad_up_weight = left_contract(normed_two, grad_up).astype(bf16)
    gain_two_sum = jnp.sum(grad_two_near * xhat_two[:half_tokens], axis=0) + jnp.sum(
        grad_two_far * xhat_two[half_tokens:], axis=0
    )
    shift_two_sum = jnp.sum(grad_two_near, axis=0) + jnp.sum(grad_two_far, axis=0)
    grad_two_other, grad_up_weight, gain_two_sum, shift_two_sum = tie(
        grad_two_other, grad_up_weight, gain_two_sum, shift_two_sum
    )
    grad_up_weight = scatter(grad_up_weight)
    grad_two_own = grad_two_near + grad_two_other.astype(f32)
    grad_hidden = grad_own.astype(f32) + norm_back(
        grad_two_own, gain_two, xhat_two[:half_tokens], rate_two[:half_tokens]
    )
    hidden_low = grad_hidden.astype(bf16)

    grad_mixed = right_contract(hidden_low, out_full).astype(bf16)
    mixed_parts = grad_mixed.reshape(half_tokens, groups, part)
    grad_heads_other = swap(pick(mixed_parts, 1, groups - 1 - side))
    late_activated, mixed_parts = lax.optimization_barrier((activated, mixed_parts))
    partial_out = matmul(late_activated, down_full)
    partial_own = partial_out[:half_tokens]
    partial_other = partial_out[half_tokens:].astype(bf16)
    grad_heads_other, partial_other, hidden_late = lax.optimization_barrier(
        (grad_heads_other, partial_other, hidden_low)
    )
    low_parts = hidden_late.reshape(half_tokens, groups, part)
    low_other = swap(pick(low_parts, 1, groups - 1 - side))
    result_other = swap(partial_other)
    grad_heads = jnp.concatenate([pick(mixed_parts, 1), grad_heads_other], axis=0)
    grad_joint = attend_back(joint, side_array, slopes, far, logs, mixed_own, grad_heads)
    grad_joint, low_other = lax.optimization_barrier((grad_joint, low_other))

    low_columns = jnp.concatenate([pick(low_parts, 1), low_other], axis=0)
    grad_out = left_contract(mixed, low_columns).astype(bf16)
    result = hidden[:half_tokens] + partial_own + result_other.astype(f32) + down_bias

    grad_joint_weight = left_contract(normed_one, grad_joint).astype(bf16)
    last = jnp.concatenate([grad_joint_weight, grad_out], axis=1)
    last = last.reshape(shards, rows, wide + part)
    grad_joint, last, grad_down = lax.optimization_barrier((grad_joint, last, grad_down))
    last = tree_step(tree_shape(last), depth - 1)
    grad_one_far = right_contract(grad_joint[half_tokens:], joint_full)
    grad_one_other = swap(grad_one_far.astype(bf16))
    grad_one_near = right_contract(grad_joint[:half_tokens], joint_full)

    def spread(x):
        empty = jnp.zeros_like(x)
        return weave(x, empty, 0).reshape(width)

    joint_sums = jnp.sum(grad_joint.astype(f32), axis=0)
    sums = [
        jnp.sum(grad_one_near * xhat_one[:half_tokens], axis=0)
        + jnp.sum(grad_one_far * xhat_one[half_tokens:], axis=0),
        jnp.sum(grad_one_near, axis=0) + jnp.sum(grad_one_far, axis=0),
        spread(joint_sums[:part]),
        spread(joint_sums[2 * part :]),
        jnp.sum(hidden_low.astype(f32), axis=0),
        gain_two_sum,
        shift_two_sum,
        jnp.sum(grad_own.astype(f32), axis=0),
    ]
    up_sums = jnp.sum(grad_up.astype(f32), axis=0).reshape(shards, unit)
    up_sums = weave(up_sums, jnp.zeros_like(up_sums), 1).reshape(shards, hidden_rows)
    sum_rows = jnp.concatenate([s.reshape(shards, rows) for s in sums] + [up_sums], axis=1)
    sum_tree = tree_shape(sum_rows[:, None])
    middle = (wide + part) // 2
    left, right = last[..., :middle], last[..., middle:]
    for turn in range(depth - 1):
        left = tree_step(left, depth - 2 - turn)
        if turn < depth - 2:
            right = tree_step(right, depth - 3 - turn)
        else:
            right = tree_step(right, depth - 2, 0)
        sum_tree = tree_step(sum_tree, depth - 1 - turn)
        if turn == 1:
            left, right, sum_tree, grad_one_other, grad_up_weight = tie(
                left, right, sum_tree, grad_one_other, grad_up_weight
            )
        else:
            left, right, sum_tree = tie(left, right, sum_tree)
    last = jnp.concatenate([left, right], axis=-1)
    last_other = swap(last)
    vector_total = tree_step(sum_tree, 0)[0]
    vector_total = vector_total + swap(vector_total)

    grad_one_own = grad_one_near + grad_one_other.astype(f32)
    grad_tokens = grad_hidden + norm_back(
        grad_one_own, gain_one, xhat_one[:half_tokens], rate_one[:half_tokens]
    )

    down_total = weave(grad_down, swap(grad_down), 0).reshape(hidden_rows, width)
    up_own = grad_up_weight.reshape(rows, shards, unit)
    up_other = swap(grad_up_weight).reshape(rows, shards, unit)
    up_total = weave(up_own, up_other, 2).reshape(rows, shards * hidden_rows)
    joint_total = weave(
        last[:, :wide].reshape(rows, 3, part), last_other[:, :wide].reshape(rows, 3, part), 2
    ).reshape(rows, 3 * width)
    out_total = weave(last[:, wide:], last_other[:, wide:], 1).reshape(rows, width)

    def total(index):
        return vector_total[index * rows : (index + 1) * rows]

    return (
        result.astype(bf16)[None],
        grad_tokens[None],
        total(0),
        total(1),
        joint_total.astype(f32),
        jnp.stack([total(2), total(3)]),
        out_total.astype(f32),
        total(4),
        total(5),
        total(6),
        up_total.astype(f32),
        vector_total[8 * rows : 8 * rows + hidden_rows],
        down_total.astype(f32),
        total(7),
    )


def solution(mesh):
    in_specs = (
        P("fsdp", "seq", None),
        P("fsdp", None),
        P("fsdp"),
        P("fsdp"),
        P("fsdp", None),
        P(None, "fsdp"),
        P("fsdp", None),
        P("fsdp"),
        P("fsdp"),
        P("fsdp"),
        P("fsdp", None),
        P("fsdp"),
        P("fsdp", None),
        P("fsdp"),
        P("fsdp", "seq", None),
    )
    out_specs = (
        P("fsdp", "seq", None),
        P("fsdp", "seq", None),
        P("fsdp"),
        P("fsdp"),
        P("fsdp", None),
        P(None, "fsdp"),
        P("fsdp", None),
        P("fsdp"),
        P("fsdp"),
        P("fsdp"),
        P("fsdp", None),
        P("fsdp"),
        P("fsdp", None),
        P("fsdp"),
    )
    return jax.shard_map(
        one_device, mesh=mesh, in_specs=in_specs, out_specs=out_specs, check_vma=False
    )
```
